32 devices in a mesh: grp: 2 (over x), seq: 8 (over z, y), head: 2 (over core).
Axes of the slice: x: 2, y: 2, z: 4, core: 2. Of those that a mesh axis runs over, the one named last changes fastest.
Arguments:
- q_feat: bfloat16 [8192, 256], P(('grp', 'seq'), 'head'), parts along dimension 0, may hold values from -5 to 5
- k_feat: bfloat16 [8192, 256], P(('grp', 'seq'), 'head'), parts along dimension 0, may hold values from -5 to 5
- values: bfloat16 [8192, 2048], P(('grp', 'seq'), 'head'), parts along dimension 0, may hold values from -8 to 8
- win_query: bfloat16 [8192, 2048], P(('grp', 'seq'), 'head'), parts along dimension 0, may hold values from -20 to 20
- win_key: bfloat16 [8192, 2048], P(('grp', 'seq'), 'head'), parts along dimension 0, may hold values from -5 to 5
- log_gates: float32 [8192, 16], P(('grp', 'seq'), 'head'), parts along dimension 0, may hold values from -2.2 to 0
- conv_weight: float32 [3, 2048], P(None, 'head'), may hold values from -2.5 to 2.5
Outputs:
- mixed: bfloat16 [8192, 2048], P(('grp', 'seq'), 'head'), parts along dimension 0
The draws below stay inside these ranges and needn't reach their ends.
There are 2 independent parts, one for each index of `grp`. The reference program is written for one: setup_inputs(seed, part) draws one part's arguments, and reference() takes and returns one part's arrays. A program takes and returns all parts, laid end to end along the dimension named above; an argument that names none is the same for every part. Nothing has to cross between parts.
All inputs are finite; a program needn't handle non-finite values.
Results may differ from the reference program's by a relative error of at most 0.011.
Values may be sent and summed in bfloat16 or wider, within the bound.
A program may use at most 192 MiB of HBM per device.

```python
import math
import jax
import jax.numpy as jnp
from jax import lax

HEADS = 16
HEAD_DIM = 128
FEAT_DIM = 16
FEATURES = 273
WINDOW = 64
CONV = 3
BLOCK = 512
TOK_DEV = 512
DOCUMENT_TOKENS = 4096


def draw_win_key(key, part):
    shape = (DOCUMENT_TOKENS, HEADS * HEAD_DIM)
    drawn = jnp.clip(jax.random.normal(jax.random.fold_in(key, 11), shape, jnp.float32), -5.0, 5.0)
    return drawn.astype(jnp.bfloat16)


def draw_win_query(key, part):
    shape = (DOCUMENT_TOKENS, HEADS * HEAD_DIM)
    drawn = jnp.clip(jax.random.normal(jax.random.fold_in(key, 13), shape, jnp.float32), -5.0, 5.0)
    return drawn.astype(jnp.bfloat16)


def draw_k_feat(key, part):
    shape = (DOCUMENT_TOKENS, HEADS * FEAT_DIM)
    pieces = DOCUMENT_TOKENS // TOK_DEV
    phase = jax.random.randint(jax.random.fold_in(key, 41), (HEADS,), 0, 2)
    piece_index = jnp.arange(pieces)
    loud = (piece_index[:, None] + phase[None, :]) % 2 == 0
    level = jnp.where(loud, 2.5, 0.25).astype(jnp.float32)
    level = jnp.repeat(jnp.repeat(level, FEAT_DIM, axis=1), TOK_DEV, axis=0)
    noise = jax.random.normal(jax.random.fold_in(key, 42), shape, jnp.float32)
    return jnp.clip(noise * level, -5.0, 5.0).astype(jnp.bfloat16)


def draw_values(key, part):
    shape = (DOCUMENT_TOKENS, HEADS * HEAD_DIM)
    drawn = 2.0 * jax.random.normal(jax.random.fold_in(key, 21), shape, jnp.float32)
    return jnp.clip(drawn, -8.0, 8.0).astype(jnp.bfloat16)


def head_classes(key):
    order = jax.random.permutation(jax.random.fold_in(key, 31), HEADS)
    count = max(1, HEADS // 4)
    fast = order < count
    medium = (order >= count) & (order < 2 * count)
    return (fast, medium)


def draw_log_gates(key, part):
    fast, medium = head_classes(key)
    pieces = DOCUMENT_TOKENS // TOK_DEV
    slow_rate = jnp.exp(jax.random.uniform(jax.random.fold_in(key, 32), (HEADS,), jnp.float32, math.log(0.02), math.log(0.11))) / DOCUMENT_TOKENS
    fast_rate = 1.0 / jnp.exp(jax.random.uniform(jax.random.fold_in(key, 33), (HEADS,), jnp.float32, math.log(30.0), math.log(50.0)))
    medium_total = jnp.exp(jax.random.uniform(jax.random.fold_in(key, 38), (HEADS,), jnp.float32, math.log(4.65), math.log(5.0)))
    multiplier = jnp.exp(jax.random.uniform(jax.random.fold_in(key, 34), (pieces, HEADS), jnp.float32, -0.7, 0.7))
    medium_factor = jnp.exp(jax.random.uniform(jax.random.fold_in(key, 37), (pieces, HEADS), jnp.float32, 0.0, math.log(2.0)))
    drawn_rate = jnp.where(fast, fast_rate, slow_rate)[None, :] * multiplier
    medium_rate = medium_total[None, :] * medium_factor / TOK_DEV
    piece_rate = jnp.where(medium[None, :], medium_rate, drawn_rate)
    rates = jnp.repeat(piece_rate, TOK_DEV, axis=0)
    spike_location = jax.random.randint(jax.random.fold_in(key, 35), (3,), 0, DOCUMENT_TOKENS)
    spike_retained = jax.random.uniform(jax.random.fold_in(key, 36), (3,), jnp.float32, 0.5, 0.8)
    token_positions = jnp.arange(DOCUMENT_TOKENS)[:, None]
    spikes_list = jnp.sum(jnp.where(token_positions == spike_location[None, :], jnp.log(spike_retained)[None, :], 0.0), axis=1, keepdims=True)
    return (-rates + spikes_list).astype(jnp.float32)


def block_levels(key, dims, cuts, low, high):
    def one(dim, blocks):
        steps = jax.random.uniform(jax.random.fold_in(jax.random.fold_in(key, 6), dim), (blocks,), jnp.float32, low / len(cuts), high / len(cuts))
        return jnp.repeat(jnp.exp(steps), dims[dim] // blocks).reshape((-1,) + (1,) * (len(dims) - dim - 1))

    gain = one(*cuts[0])
    for cut in cuts[1:]:
        gain = gain * one(*cut)
    return gain


def normal_values(key, shape, scale, most, cuts=(), kind=jnp.bfloat16):
    entries = jax.random.normal(key, shape, jnp.float32) * scale
    if len(cuts) > 0:
        entries = block_levels(key, shape, cuts, -0.22, 0.18) * entries
    return jnp.clip(entries, min=-most, max=most).astype(kind)


def setup_inputs(seed: int = 0, part: int = 0) -> dict:
    seeds = jax.random.split(jax.random.key(seed), 8)
    part_splits = jax.random.split(jax.random.fold_in(seeds[7], part), 8)
    return {
        "q_feat": normal_values(part_splits[0], (DOCUMENT_TOKENS, HEADS * FEAT_DIM), 2.0, 5.0, ((0, 8), (1, 2))),
        "k_feat": draw_k_feat(jax.random.fold_in(jax.random.fold_in(seeds[7], part), 71), part),
        "values": draw_values(jax.random.fold_in(jax.random.fold_in(seeds[7], part), 71), part),
        "win_query": draw_win_query(jax.random.fold_in(jax.random.fold_in(seeds[7], part), 71), part),
        "win_key": draw_win_key(jax.random.fold_in(jax.random.fold_in(seeds[7], part), 71), part),
        "log_gates": draw_log_gates(jax.random.fold_in(jax.random.fold_in(seeds[7], part), 71), part),
        "conv_weight": normal_values(seeds[6], (CONV, HEADS * HEAD_DIM), 0.6, 2.5, ((1, 2),), jnp.float32),
    }


def taylor_map(features, heads):
    tok_rows = features.shape[0]
    width = features.shape[1] // heads
    spread = features.astype(jnp.float32).reshape(tok_rows, heads, width)
    linear = spread * width ** -0.25
    square = (spread[:, :, :, None] * spread[:, :, None, :]).reshape(tok_rows, heads, width * width) * (2.0 * width) ** -0.5
    ones = jnp.ones((tok_rows, heads, 1), jnp.float32)
    return jnp.concatenate([ones, linear, square], axis=2).astype(jnp.bfloat16)


def reference(q_feat, k_feat, values, win_query, win_key, log_gates, conv_weight):
    maximum_level = lax.Precision.HIGHEST
    count = DOCUMENT_TOKENS // BLOCK
    channels = HEADS * HEAD_DIM

    def split(array):
        return array.reshape((count, BLOCK) + array.shape[1:])

    block_inputs = (split(q_feat), split(k_feat), split(values), split(win_query), split(win_key), split(log_gates), jnp.arange(count, dtype=jnp.int32))
    start_carry = (jnp.zeros((HEADS, FEATURES, HEAD_DIM), jnp.float32), jnp.zeros((HEADS, FEATURES), jnp.float32),
                   jnp.zeros((WINDOW, channels), jnp.bfloat16), jnp.zeros((WINDOW, channels), jnp.bfloat16))
    causal = jnp.arange(BLOCK)[:, None] >= jnp.arange(BLOCK)[None, :]
    query_pos = jnp.arange(BLOCK)[:, None]
    key_pos = jnp.arange(BLOCK + WINDOW)[None, :] - WINDOW

    def advance(carry, inputs):
        running_state, norm_total, prev_key, prev_value = carry
        query_block, key_block, value_block, wq_block, wk_block, gate_block, index = inputs
        value_ext = jnp.concatenate([prev_value, value_block], axis=0)
        key_ext = jnp.concatenate([prev_key, wk_block], axis=0)
        convolved = jnp.zeros((BLOCK, channels), jnp.float32)
        for tap in range(CONV):
            convolved = convolved + conv_weight[tap][None, :] * value_ext[WINDOW - tap: WINDOW - tap + BLOCK].astype(jnp.float32)
        filtered_values = convolved.astype(jnp.bfloat16).reshape(BLOCK, HEADS, HEAD_DIM).astype(jnp.float32)
        query_features = taylor_map(query_block, HEADS).astype(jnp.float32)
        key_features = taylor_map(key_block, HEADS).astype(jnp.float32)
        cumulative = jnp.cumsum(gate_block, axis=0)
        cum_heads = cumulative.T
        decay_factor = jnp.exp(jnp.where(causal[None], cum_heads[:, :, None] - cum_heads[:, None, :], -jnp.inf))
        score_matrix = jnp.einsum("sjz,djz->jsd", query_features, key_features, precision=maximum_level) * decay_factor
        denominator = jnp.sum(score_matrix, axis=2).T
        numerator = jnp.einsum("hqk,khd->qhd", score_matrix.astype(jnp.bfloat16).astype(jnp.float32), filtered_values, precision=maximum_level)
        entering = jnp.exp(cumulative)
        numerator = numerator + entering[:, :, None] * jnp.einsum("qhf,hfd->qhd", query_features, running_state, precision=maximum_level)
        denominator = denominator + entering * jnp.einsum("qhf,hf->qh", query_features, norm_total, precision=maximum_level)
        linear = numerator / denominator[:, :, None]
        block_finish = cumulative[-1]
        retention = jnp.exp(block_finish[None, :] - cumulative)
        key_expanded = key_features * retention[:, :, None]
        running_state = jnp.exp(block_finish)[:, None, None] * running_state + jnp.einsum("mwv,mwr->wvr", key_expanded, filtered_values, precision=maximum_level)
        norm_total = jnp.exp(block_finish)[:, None] * norm_total + jnp.sum(key_expanded, axis=0)
        win_keys = key_ext.reshape(BLOCK + WINDOW, HEADS, HEAD_DIM).astype(jnp.float32)
        win_values = value_ext.reshape(BLOCK + WINDOW, HEADS, HEAD_DIM).astype(jnp.float32)
        win_queries = wq_block.reshape(BLOCK, HEADS, HEAD_DIM).astype(jnp.float32)
        win_scores = jnp.einsum("qhd,khd->hqk", win_queries, win_keys, precision=maximum_level) * HEAD_DIM ** -0.5
        valid = (key_pos <= query_pos) & (key_pos > query_pos - WINDOW) & (index * BLOCK + key_pos >= 0)
        win_scores = jnp.where(valid[None], win_scores, -jnp.inf)
        top = jnp.max(win_scores, axis=2, keepdims=True)
        weights = jnp.exp(win_scores - top)
        total = jnp.sum(weights, axis=2, keepdims=True)
        probs = (weights / total).astype(jnp.bfloat16).astype(jnp.float32)
        window_out = jnp.einsum("hqk,khd->qhd", probs, win_values, precision=maximum_level)
        mixed = (linear + window_out).astype(jnp.bfloat16).reshape(BLOCK, channels)
        return (running_state, norm_total, wk_block[BLOCK - WINDOW:], value_block[BLOCK - WINDOW:]), mixed

    final_carry, outputs = lax.scan(advance, start_carry, block_inputs)
    return outputs.reshape(DOCUMENT_TOKENS, channels)
```

```python
import functools

import jax
import jax.numpy as jnp
from jax import lax
from jax.experimental import pallas as pl
from jax.experimental.pallas import tpu as pltpu
from jax.sharding import PartitionSpec as P

WINDOW = 64
TILE = 128
FOLDED = 160
F32 = jnp.float32
BF16 = jnp.bfloat16
MESH = pl.DeviceIdType.MESH


def dot(a, b):
    return lax.dot_general(a, b, (((1,), (0,)), ((), ())), preferred_element_type=F32)


def dot_t(a, b):
    return lax.dot_general(a, b, (((1,), (1,)), ((), ())), preferred_element_type=F32)


def dot_first(a, b):
    return lax.dot_general(a, b, (((0,), (0,)), ((), ())), preferred_element_type=F32)


def fold_features(x, square_scale, pair_scale, linear_scale):
    rows = lax.broadcasted_iota(jnp.int32, x.shape, 0)
    scaled = x * pair_scale
    parts = [(x * square_scale) * x]
    for step in range(1, 8):
        parts.append(scaled * pltpu.roll(x, 16 - step, 0))
    half = scaled * pltpu.roll(x, 8, 0)
    parts.append(jnp.where(rows < 8, half, jnp.where(rows == 8, 1.0, 0.0)))
    parts.append(x * linear_scale)
    return jnp.concatenate([part.astype(BF16) for part in parts], axis=0)


def kernel(
    n, heads, size, width,
    qf, kf, gates, weight, values, win_key, win_query,
    out,
    vx, kx, wq, halo, vf, vw, qt, kt, phik, phiq, numden, win, ccol, crow,
    s_send, s_recv, side, e_send, e_recv,
    in_sem, halo_send, halo_recv, ss_sem, sr_sem, ds_sem, dr_sem, es_sem, er_sem,
):
    me = lax.axis_index("seq")
    tok = qf.shape[0]
    per_head = n // heads
    rows = FOLDED // per_head
    tiles = tok // TILE
    tail = WINDOW

    load_v = pltpu.make_async_copy(values, vx.at[pl.ds(tail, tok)], in_sem.at[0])
    load_k = pltpu.make_async_copy(win_key, kx.at[pl.ds(tail, tok)], in_sem.at[1])
    load_q = pltpu.make_async_copy(win_query, wq, in_sem.at[2])
    load_v.start()
    load_k.start()
    load_q.start()

    barrier = pltpu.get_barrier_semaphore()
    for peer in range(n):
        @pl.when(peer != me)
        def _(peer=peer):
            pl.semaphore_signal(barrier, inc=1, device_id={"seq": peer}, device_id_type=MESH)

    @pl.when(me == 0)
    def _():
        vx[0:tail, :] = jnp.zeros((tail, heads * size), BF16)
        kx[0:tail, :] = jnp.zeros((tail, heads * size), BF16)
        halo[...] = jnp.zeros(halo.shape, BF16)

    nxt = lax.rem(me + 1, n)

    def halo_copies():
        short = pltpu.make_async_remote_copy(
            values.at[pl.ds(tok - 16, 16)], halo, halo_send.at[0], halo_recv.at[0],
            device_id={"seq": nxt}, device_id_type=MESH)
        long_v = pltpu.make_async_remote_copy(
            values.at[pl.ds(tok - tail, tail)], vx.at[pl.ds(0, tail)], halo_send.at[1], halo_recv.at[1],
            device_id={"seq": nxt}, device_id_type=MESH)
        long_k = pltpu.make_async_remote_copy(
            win_key.at[pl.ds(tok - tail, tail)], kx.at[pl.ds(0, tail)], halo_send.at[2], halo_recv.at[2],
            device_id={"seq": nxt}, device_id_type=MESH)
        return short, long_v, long_k

    def s_copy(block):
        return pltpu.make_async_remote_copy(
            s_send.at[block], s_recv.at[me], ss_sem.at[block], sr_sem.at[me],
            device_id={"seq": block}, device_id_type=MESH)

    def s_arrival(source):
        return pltpu.make_async_remote_copy(
            s_send.at[source], s_recv.at[source], ss_sem.at[source], sr_sem.at[source],
            device_id={"seq": source}, device_id_type=MESH)

    def d_copy(peer):
        return pltpu.make_async_remote_copy(
            side.at[me], side.at[me], ds_sem.at[peer], dr_sem.at[me],
            device_id={"seq": peer}, device_id_type=MESH)

    def d_arrival(source):
        return pltpu.make_async_remote_copy(
            side.at[source], side.at[source], ds_sem.at[source], dr_sem.at[source],
            device_id={"seq": source}, device_id_type=MESH)

    def e_copy(peer):
        return pltpu.make_async_remote_copy(
            e_send.at[peer], e_recv.at[me], es_sem.at[peer], er_sem.at[me],
            device_id={"seq": peer}, device_id_type=MESH)

    def e_arrival(source):
        return pltpu.make_async_remote_copy(
            e_send.at[source], e_recv.at[source], es_sem.at[source], er_sem.at[source],
            device_id={"seq": source}, device_id_type=MESH)

    before_or_at = jnp.where(
        lax.broadcasted_iota(jnp.int32, (tok, tok), 0) <= lax.broadcasted_iota(jnp.int32, (tok, tok), 1),
        1.0, 0.0).astype(BF16)
    upper = gates[...].astype(BF16)
    rest = gates[...] - upper.astype(F32)
    middle = rest.astype(BF16)
    lowest = (rest - middle.astype(F32)).astype(BF16)
    total = dot(jnp.concatenate([upper, middle, lowest], axis=0), before_or_at)
    total = total[0:heads] + (total[heads:2 * heads] + total[2 * heads:3 * heads])
    crow[...] = total
    ccol[...] = jnp.concatenate([total, jnp.zeros((128 - heads, tok), F32)], axis=0).T
    kt[...] = kf[...].astype(F32).T
    qt[...] = qf[...].astype(F32).T
    keep_row = jnp.exp(crow[:, tok - 1:tok] - crow[...])
    keep_hi = keep_row.astype(BF16)
    keep_lo = (keep_row - keep_hi.astype(F32)).astype(BF16)
    finish = jnp.exp(crow[:, tok - 1:tok])

    pl.semaphore_wait(barrier, n - 1)

    @pl.when(me < n - 1)
    def _():
        for copy in halo_copies():
            copy.start()

    for h in range(heads):
        phik[h] = fold_features(kt[h * width:(h + 1) * width, :], 1.0, 1.0, 1.0)
    load_v.wait()

    @pl.when(me > 0)
    def _():
        halo_copies()[0].wait_recv()

    head_row = lax.broadcasted_iota(jnp.int32, (heads, FOLDED), 0)
    norm = jnp.zeros((heads, FOLDED), F32)
    for h in range(heads):
        lanes = slice(h * size, (h + 1) * size)
        current = vx[tail:tail + tok, lanes].astype(F32)
        vf[8:8 + tok, lanes] = current
        vf[0:8, lanes] = halo[:, lanes].astype(F32)[8:16, :]
        conv = weight[0:1, lanes] * current
        for tap in range(1, weight.shape[0]):
            conv = conv + weight[tap:tap + 1, lanes] * vf[8 - tap:8 - tap + tok, lanes]
        conv = conv.astype(BF16)
        vw[h, :, 0:size] = conv
        vw[h, :, size:2 * size] = jnp.ones((tok, size), BF16)
        column = ccol[:, h:h + 1]
        keep = jnp.exp(ccol[tok - 1:tok, h:h + 1] - column)
        state = dot(phik[h], (conv.astype(F32) * keep).astype(BF16))
        norm_h = dot_t(keep_hi, phik[h]) + dot_t(keep_lo, phik[h])
        norm = jnp.where(head_row == h, norm_h, norm)
        for b in range(per_head):
            block = h * per_head + b
            s_send[block] = state[b * rows:(b + 1) * rows, :].astype(BF16)
        if h + 1 in (heads // 2, heads):
            half = n // 2
            start = 0 if h + 1 == heads // 2 else half
            for turn in range(half):
                peer = start + lax.rem(me + turn, half)

                @pl.when((peer != me) & (me < n - 1))
                def _(peer=peer):
                    s_copy(peer).start()

    side[me] = jnp.concatenate([norm, jnp.broadcast_to(finish, (heads, 256 - FOLDED))], axis=1)

    @pl.when(me < n - 1)
    def _():
        for offset in range(1, n):
            d_copy(lax.rem(me + offset, n)).start()

    s_recv[me] = s_send[me]

    lane_head = lax.broadcasted_iota(jnp.int32, (tok, heads * width), 1) // width
    kt_narrow = kt[...].astype(BF16)
    q_quarter = qf[...] * jnp.asarray(0.25, BF16)
    diagonal = (lax.broadcasted_iota(jnp.int32, (TILE, TILE), 0)
                >= lax.broadcasted_iota(jnp.int32, (TILE, TILE), 1))
    for h in range(heads):
        lone = jnp.where(lane_head == h, q_quarter, jnp.zeros_like(q_quarter))
        for i in range(tiles):
            t0 = i * TILE
            reach = t0 + TILE
            x = dot(lone[t0:reach, :], kt_narrow[:, 0:reach])
            poly = 1.0 + x * (1.0 + 0.5 * x)
            gap = ccol[t0:reach, h:h + 1] - crow[h:h + 1, 0:reach]
            last = jnp.where(diagonal, gap[:, t0:reach], -1e30)
            if i > 0:
                gap = jnp.concatenate([gap[:, 0:t0], last], axis=1)
            else:
                gap = last
            score = (poly * jnp.exp(gap)).astype(BF16)
            numden[h, t0:reach, :] = dot(score, vw[h, 0:reach, :])

    load_k.wait()
    load_q.wait()

    @pl.when(me > 0)
    def _():
        halo_copies()[1].wait_recv()
        halo_copies()[2].wait_recv()

    r = lax.broadcasted_iota(jnp.int32, (WINDOW, 2 * WINDOW), 0)
    j = lax.broadcasted_iota(jnp.int32, (WINDOW, 2 * WINDOW), 1)
    band = (j > r) & (j <= r + WINDOW)
    steps = tok // WINDOW
    bias = jnp.where(band, 0.0, -1e30)
    bias = jnp.concatenate(
        [jnp.where(band & ((j >= WINDOW) | (me > 0)), 0.0, -1e30)] + [bias] * (steps - 1), axis=0)
    scale = size ** (-0.5)
    ones = jnp.ones((2 * WINDOW, size), BF16)

    def slide(h):
        lanes = slice(h * size, (h + 1) * size)
        s = jnp.concatenate([
            dot_t(wq[i * WINDOW:(i + 1) * WINDOW, lanes], kx[i * WINDOW:(i + 2) * WINDOW, lanes])
            for i in range(steps)], axis=0)
        s = s * scale + bias
        p = jnp.exp(s - jnp.max(s, axis=1, keepdims=True)).astype(BF16)
        pv = jnp.concatenate([
            dot(p[i * WINDOW:(i + 1) * WINDOW, :],
                jnp.concatenate([vx[i * WINDOW:(i + 2) * WINDOW, lanes], ones], axis=1))
            for i in range(steps)], axis=0)
        win[:, lanes] = pv[:, 0:size] / pv[:, size:2 * size]

    for h in range(heads // 2):
        slide(h)

    for source in range(n - 1):
        @pl.when(source != me)
        def _(source=source):
            s_arrival(source).wait_recv()
            d_arrival(source).wait_recv()

    mine = me // per_head
    running = jnp.zeros((rows, size), F32)
    e_send[0] = running.astype(BF16)
    for i in range(n - 1):
        fade = side[i, pl.ds(mine, 1), :][:, 192:193]
        running = fade * running + s_recv[i].astype(F32)
        e_send[i + 1] = running.astype(BF16)

    e_recv[me] = e_send[me]
    for offset in range(1, n):
        peer = lax.rem(me + offset, n)

        @pl.when(peer > 0)
        def _(peer=peer):
            e_copy(peer).start()

    @pl.when(me == 0)
    def _():
        e_recv[...] = jnp.zeros(e_recv.shape, BF16)

    norm_before = jnp.zeros((heads, 256), F32)
    for i in range(n - 1):
        block = side[i]
        joined = block[:, 192:193] * norm_before + block
        norm_before = jnp.where(i < me, joined, norm_before)
    norm_col = jnp.concatenate([norm_before, jnp.zeros((128 - heads, 256), F32)], axis=0).T

    for h in range(heads // 2, heads):
        slide(h)

    for h in range(heads):
        phiq[h] = fold_features(qt[h * width:(h + 1) * width, :], 1.0 / 32, 1.0 / 16, 0.25)

    for source in range(n):
        @pl.when((source != me) & (me > 0))
        def _(source=source):
            e_arrival(source).wait_recv()

    for h in range(heads):
        lanes = slice(h * size, (h + 1) * size)
        before = jnp.concatenate([e_recv[h * per_head + b] for b in range(per_head)], axis=0)
        norm_wide = jnp.broadcast_to(norm_col[0:FOLDED, h:h + 1], (FOLDED, size)).astype(BF16)
        both = dot_first(phiq[h], jnp.concatenate([before, norm_wide], axis=1))
        both = numden[h] + jnp.exp(ccol[:, h:h + 1]) * both
        out[:, lanes] = (both[:, 0:size] / both[:, size:2 * size] + win[:, lanes]).astype(BF16)

    @pl.when(me < n - 1)
    def _():
        for copy in halo_copies():
            copy.wait_send()

    for peer in range(n):
        @pl.when((peer != me) & (me < n - 1))
        def _(peer=peer):
            s_copy(peer).wait_send()
            d_copy(peer).wait_send()

        if peer > 0:
            @pl.when(peer != me)
            def _(peer=peer):
                e_copy(peer).wait_send()


def solution(mesh):
    n = mesh.shape["seq"]

    def local(q_feat, k_feat, values, win_query, win_key, log_gates, conv_weight):
        tok, channels = values.shape
        heads = log_gates.shape[1]
        size = channels // heads
        width = q_feat.shape[1] // heads
        rows = FOLDED * heads // n
        vmem = pl.BlockSpec(memory_space=pltpu.VMEM)
        anywhere = pl.BlockSpec(memory_space=pltpu.HBM)
        dma = pltpu.SemaphoreType.DMA
        return pl.pallas_call(
            functools.partial(kernel, n, heads, size, width),
            out_shape=jax.ShapeDtypeStruct((tok, channels), BF16),
            in_specs=[vmem] * 4 + [anywhere] * 3,
            out_specs=vmem,
            scratch_shapes=[
                pltpu.VMEM((tok + WINDOW, channels), BF16),
                pltpu.VMEM((tok + WINDOW, channels), BF16),
                pltpu.VMEM((tok, channels), BF16),
                pltpu.VMEM((16, channels), BF16),
                pltpu.VMEM((tok + 8, channels), F32),
                pltpu.VMEM((heads, tok, 2 * size), BF16),
                pltpu.VMEM((heads * width, tok), F32),
                pltpu.VMEM((heads * width, tok), F32),
                pltpu.VMEM((heads, FOLDED, tok), BF16),
                pltpu.VMEM((heads, FOLDED, tok), BF16),
                pltpu.VMEM((heads, tok, 2 * size), F32),
                pltpu.VMEM((tok, channels), F32),
                pltpu.VMEM((tok, 128), F32),
                pltpu.VMEM((heads, tok), F32),
                pltpu.VMEM((n, rows, size), BF16),
                pltpu.VMEM((n, rows, size), BF16),
                pltpu.VMEM((n, heads, 256), F32),
                pltpu.VMEM((n, rows, size), BF16),
                pltpu.VMEM((n, rows, size), BF16),
                dma((3,)), dma((3,)), dma((3,)),
                dma((n,)), dma((n,)), dma((n,)), dma((n,)), dma((n,)), dma((n,)),
            ],
            compiler_params=pltpu.CompilerParams(
                collective_id=0, has_side_effects=True, vmem_limit_bytes=40 * 1024 * 1024),
        )(*[pltpu.with_memory_space_constraint(x, pltpu.HBM) for x in (q_feat, k_feat, log_gates.T, conv_weight, values, win_key, win_query)])

    shard = P(("grp", "seq"), "head")
    return jax.shard_map(
        local, mesh=mesh, in_specs=(shard,) * 6 + (P(None, "head"),), out_specs=shard, check_vma=False)
```

```python
import functools

import jax
import jax.numpy as jnp
from jax import lax
from jax.experimental import pallas as pl
from jax.experimental.pallas import tpu as pltpu
from jax.sharding import PartitionSpec as P

WINDOW = 64
TILE = 128
FOLDED = 160
SLAB = 128
NORM_A, NORM_B, FADE_HI, FADE_LO = 9, 10, 11, 12
F32 = jnp.float32
BF16 = jnp.bfloat16
MESH = pl.DeviceIdType.MESH


def dot(a, b):
    return lax.dot_general(a, b, (((1,), (0,)), ((), ())), preferred_element_type=F32)


def dot_t(a, b):
    return lax.dot_general(a, b, (((1,), (1,)), ((), ())), preferred_element_type=F32)


def dot_first(a, b):
    return lax.dot_general(a, b, (((0,), (0,)), ((), ())), preferred_element_type=F32)


def fold_features(x, level, square_scale, pair_scale, linear_scale):
    rows = lax.broadcasted_iota(jnp.int32, x.shape, 0)
    levelled = x * level
    scaled = levelled * pair_scale
    parts = [(levelled * square_scale) * x]
    for step in range(1, 8):
        parts.append(scaled * pltpu.roll(x, 16 - step, 0))
    half = scaled * pltpu.roll(x, 8, 0)
    parts.append(jnp.where(rows < 8, half, jnp.where(rows == 8, level, 0.0)))
    parts.append(levelled * linear_scale)
    return jnp.concatenate([part.astype(BF16) for part in parts], axis=0)


def kernel(
    n, group, heads, size, width,
    q_feat, k_feat, log_gates, conv_weight, values, win_key, win_query,
    out,
    qf, kf, gates, weight,
    vx, kx, wq, halo, vf, vw, qt, kt, phik, phiq, numden, win, ccol, crow,
    main, s_send, s_recv, e_group, faded, before_group, t_send, t_recv, e_send, e_recv,
    in_sem, halo_send, halo_recv, ss_sem, sr_sem, ts_sem, tr_sem, es_sem, er_sem,
):
    me = lax.axis_index("seq")
    groups = n // group
    per = heads // group
    g = me // group
    r = lax.rem(me, group)
    tok = qf.shape[0]
    tiles = tok // TILE
    tail = WINDOW

    loads = [
        pltpu.make_async_copy(log_gates, gates, in_sem.at[0]),
        pltpu.make_async_copy(k_feat, kf, in_sem.at[1]),
        pltpu.make_async_copy(values, vx.at[pl.ds(tail, tok)], in_sem.at[2]),
        pltpu.make_async_copy(conv_weight, weight, in_sem.at[3]),
        pltpu.make_async_copy(q_feat, qf, in_sem.at[4]),
        pltpu.make_async_copy(win_key, kx.at[pl.ds(tail, tok)], in_sem.at[5]),
        pltpu.make_async_copy(win_query, wq, in_sem.at[6]),
    ]
    for load in loads:
        load.start()
    load_g, load_kf, load_v, load_w, load_qf, load_k, load_q = loads

    barrier = pltpu.get_barrier_semaphore()

    def greet(peer):
        pl.semaphore_signal(barrier, inc=1, device_id={"seq": peer}, device_id_type=MESH)

    for turn in range(1, group):
        greet(g * group + lax.rem(r + turn, group))
    for turn in range(1, groups):
        greet(lax.rem(me + turn * group, n))
    across_next = (r == group - 1) & (g < groups - 1)
    across_prev = (r == 0) & (g > 0)

    @pl.when(across_next)
    def _():
        greet(me + 1)

    @pl.when(across_prev)
    def _():
        greet(me - 1)

    @pl.when(me == 0)
    def _():
        vx[0:tail, :] = jnp.zeros((tail, heads * size), BF16)
        kx[0:tail, :] = jnp.zeros((tail, heads * size), BF16)
        halo[...] = jnp.zeros(halo.shape, BF16)
        e_recv[...] = jnp.zeros(e_recv.shape, BF16)

    vf[0:8, :] = jnp.zeros((8, heads * size), F32)
    nxt = lax.rem(me + 1, n)

    def halo_copy(which):
        source, target = (
            (values.at[pl.ds(tok - 16, 16)], halo),
            (values.at[pl.ds(tok - tail, tail)], vx.at[pl.ds(0, tail)]),
            (win_key.at[pl.ds(tok - tail, tail)], kx.at[pl.ds(0, tail)]),
        )[which]
        return pltpu.make_async_remote_copy(
            source, target, halo_send.at[which], halo_recv.at[which],
            device_id={"seq": nxt}, device_id_type=MESH)

    def s_copy(h):
        return pltpu.make_async_remote_copy(
            s_send.at[h], s_recv.at[h // group, r], ss_sem.at[h], sr_sem.at[h // group, r],
            device_id={"seq": g * group + h % group}, device_id_type=MESH)

    def s_arrival(c, source):
        return pltpu.make_async_remote_copy(
            s_send.at[c * group], s_recv.at[c, source], ss_sem.at[c * group], sr_sem.at[c, source],
            device_id={"seq": g * group + source}, device_id_type=MESH)

    def t_copy(c, target):
        return pltpu.make_async_remote_copy(
            t_send.at[c], t_recv.at[c, g], ts_sem.at[c, target], tr_sem.at[c, g],
            device_id={"seq": target * group + r}, device_id_type=MESH)

    def t_arrival(c, source):
        return pltpu.make_async_remote_copy(
            t_send.at[c], t_recv.at[c, source], ts_sem.at[c, source], tr_sem.at[c, source],
            device_id={"seq": source * group + r}, device_id_type=MESH)

    def e_copy(c, target):
        return pltpu.make_async_remote_copy(
            e_send.at[c, target], e_recv.at[c * group + r], es_sem.at[c, target], er_sem.at[c * group + r],
            device_id={"seq": g * group + target}, device_id_type=MESH)

    def e_arrival(h):
        return pltpu.make_async_remote_copy(
            e_send.at[0, 0], e_recv.at[h], es_sem.at[0, 0], er_sem.at[h],
            device_id={"seq": g * group + h % group}, device_id_type=MESH)

    before_or_at = jnp.where(
        lax.broadcasted_iota(jnp.int32, (tok, tok), 0) <= lax.broadcasted_iota(jnp.int32, (tok, tok), 1),
        1.0, 0.0).astype(BF16)
    load_g.wait()
    upper = gates[...].astype(BF16)
    rest = gates[...] - upper.astype(F32)
    middle = rest.astype(BF16)
    lowest = (rest - middle.astype(F32)).astype(BF16)
    total = dot(jnp.concatenate([upper, middle, lowest], axis=0), before_or_at)
    total = total[0:heads] + (total[heads:2 * heads] + total[2 * heads:3 * heads])
    crow[...] = total
    ccol[...] = jnp.concatenate([total, jnp.zeros((128 - heads, tok), F32)], axis=0).T
    keep_row = jnp.exp(total[:, tok - 1:tok] - total)
    finish = jnp.exp(total[:, tok - 1:tok])
    finish_hi = finish.astype(BF16).astype(F32)
    finish_lo = finish - finish_hi

    load_kf.wait()
    kt[...] = kf[...].astype(F32).T
    for h in range(heads):
        phik[h] = fold_features(
            kt[h * width:(h + 1) * width, :], keep_row[h:h + 1, :], 1.0, 1.0, 1.0)

    load_w.wait()
    load_v.wait()
    slab_row = lax.broadcasted_iota(jnp.int32, (16, size), 0)
    ones_rows = jnp.ones((16, tok), BF16)

    def state(h):
        lanes = slice(h * size, (h + 1) * size)
        current = vx[tail:tail + tok, lanes].astype(F32)
        vf[8:8 + tok, lanes] = current
        conv = weight[0:1, lanes] * current
        for tap in range(1, weight.shape[0]):
            conv = conv + weight[tap:tap + 1, lanes] * vf[8 - tap:8 - tap + tok, lanes]
        conv = conv.astype(BF16)
        vw[h, :, 0:size] = conv
        vw[h, :, size:2 * size] = jnp.ones((tok, size), BF16)
        folded = dot(phik[h], conv)
        norm = dot_t(ones_rows, phik[h])
        norm_b = jnp.concatenate([norm[:, SLAB:FOLDED], jnp.zeros((16, 2 * SLAB - FOLDED), F32)], axis=1)
        slab = folded[SLAB:SLAB + 16, :]
        slab = jnp.where(slab_row == NORM_A, norm[:, 0:SLAB], slab)
        slab = jnp.where(slab_row == NORM_B, norm_b, slab)
        slab = jnp.where(slab_row == FADE_HI, finish_hi[h:h + 1, :], slab)
        slab = jnp.where(slab_row == FADE_LO, finish_lo[h:h + 1, :], slab)
        main[h] = jnp.concatenate([folded[0:SLAB, :], slab, folded[SLAB + 16:, :]], axis=0)

    state(0)
    pl.semaphore_wait(
        barrier, (group - 1) + (groups - 1) + across_next.astype(jnp.int32) + across_prev.astype(jnp.int32))

    @pl.when(me < n - 1)
    def _():
        halo_copy(0).start()
        halo_copy(1).start()

    for h in range(1, heads):
        state(h)

    @pl.when(me > 0)
    def _():
        halo_copy(0).wait_recv()

    vf[0:8, :] = halo[...].astype(F32)[8:16, :]
    first = weight[0:1, :] * vf[8:24, :]
    for tap in range(1, weight.shape[0]):
        first = first + weight[tap:tap + 1, :] * vf[8 - tap:24 - tap, :]
    first = first.astype(BF16)
    for h in range(heads):
        lanes = slice(h * size, (h + 1) * size)
        change = first[:, lanes].astype(F32) - vw[h, 0:16, 0:size].astype(F32)
        vw[h, 0:16, 0:size] = first[:, lanes]
        change = jnp.concatenate([change.astype(BF16), jnp.zeros((TILE - 16, size), BF16)], axis=0)
        s_send[h] = (main[h] + dot(phik[h, :, 0:TILE], change)).astype(BF16)

        @pl.when((r != h % group) & (me < n - 1))
        def _(h=h):
            s_copy(h).start()

    for c in range(per):
        s_recv[c, r] = s_send[c * group + r]

    @pl.when(me < n - 1)
    def _():
        halo_copy(2).start()

    lane_head = lax.broadcasted_iota(jnp.int32, (tok, heads * width), 1) // width
    load_qf.wait()
    kt_narrow = kt[...].astype(BF16)
    q_quarter = qf[...] * jnp.asarray(0.25, BF16)
    diagonal = (lax.broadcasted_iota(jnp.int32, (TILE, TILE), 0)
                >= lax.broadcasted_iota(jnp.int32, (TILE, TILE), 1))

    def scores(h):
        lone = jnp.where(lane_head == h, q_quarter, jnp.zeros_like(q_quarter))
        for i in range(tiles):
            t0 = i * TILE
            reach = t0 + TILE
            x = dot(lone[t0:reach, :], kt_narrow[:, 0:reach])
            poly = 1.0 + x * (1.0 + 0.5 * x)
            gap = ccol[t0:reach, h:h + 1] - crow[h:h + 1, 0:reach]
            last = jnp.where(diagonal, gap[:, t0:reach], -1e30)
            if i > 0:
                gap = jnp.concatenate([gap[:, 0:t0], last], axis=1)
            else:
                gap = last
            score = (poly * jnp.exp(gap)).astype(BF16)
            numden[h, t0:reach, :] = dot(score, vw[h, 0:reach, :])

    def fade_of(block):
        slab = block[SLAB:SLAB + 16, :]
        return slab[FADE_HI:FADE_HI + 1, :] + slab[FADE_LO:FADE_LO + 1, :]

    def emit(c, earlier):
        for i in range(group):
            entering = e_group[c, i]
            if earlier is not None:
                entering = entering + faded[c * group + i] * earlier
            e_send[c, i] = entering.astype(BF16)
        e_recv[c * group + r] = e_send[c, r]
        for turn in range(1, group):
            target = lax.rem(r + turn, group)

            @pl.when((g > 0) | (target > 0))
            def _(target=target):
                e_copy(c, target).start()

    def gather(c):
        for j in range(group):
            @pl.when((j != r) & (g * group + j < n - 1))
            def _(j=j):
                s_arrival(c, j).wait_recv()

        running = jnp.zeros((FOLDED, size), F32)
        fades = jnp.ones((1, size), F32)
        for j in range(group):
            e_group[c, j] = running
            faded[c * group + j] = fades
            block = s_recv[c, j].astype(F32)
            fade = fade_of(block)
            running = fade * running + block
            fades = fades * fade

        if groups > 1:
            fades_hi = fades.astype(BF16).astype(F32)
            slab = jnp.where(slab_row == FADE_HI, fades_hi, running[SLAB:SLAB + 16, :])
            slab = jnp.where(slab_row == FADE_LO, fades - fades_hi, slab)
            t_send[c] = jnp.concatenate(
                [running[0:SLAB, :], slab, running[SLAB + 16:, :]], axis=0).astype(BF16)
            for target in range(1, groups):
                @pl.when(target > g)
                def _(target=target):
                    t_copy(c, target).start()

        @pl.when(g == 0)
        def _():
            emit(c, None)

    def pass_on(c):
        @pl.when(g > 0)
        def _():
            before_group[...] = jnp.zeros(before_group.shape, F32)
            for source in range(groups - 1):
                @pl.when(source < g)
                def _(source=source):
                    t_arrival(c, source).wait_recv()
                    block = t_recv[c, source].astype(F32)
                    before_group[...] = fade_of(block) * before_group[...] + block
            emit(c, before_group[...])

    row = lax.broadcasted_iota(jnp.int32, (WINDOW, 2 * WINDOW), 0)
    col = lax.broadcasted_iota(jnp.int32, (WINDOW, 2 * WINDOW), 1)
    band = (col > row) & (col <= row + WINDOW)
    steps = tok // WINDOW
    scale = size ** (-0.5)
    ones = jnp.ones((2 * WINDOW, size), BF16)

    def slide(h, start, stop, bias):
        lanes = slice(h * size, (h + 1) * size)
        s = jnp.concatenate([
            dot_t(wq[i * WINDOW:(i + 1) * WINDOW, lanes], kx[i * WINDOW:(i + 2) * WINDOW, lanes])
            for i in range(start, stop)], axis=0)
        s = s * scale + bias
        p = jnp.exp(s - jnp.max(s, axis=1, keepdims=True)).astype(BF16)
        pv = jnp.concatenate([
            dot(p[(i - start) * WINDOW:(i - start + 1) * WINDOW, :],
                jnp.concatenate([vx[i * WINDOW:(i + 2) * WINDOW, lanes], ones], axis=1))
            for i in range(start, stop)], axis=0)
        win[start * WINDOW:stop * WINDOW, lanes] = pv[:, 0:size] / pv[:, size:2 * size]

    for h in range(0, heads - 2):
        scores(h)
    gather(0)
    for h in range(heads - 2, heads):
        scores(h)
    for c in range(1, per):
        gather(c)

    load_k.wait()
    load_q.wait()
    bias = jnp.concatenate([jnp.where(band, 0.0, -1e30)] * (steps - 1), axis=0)
    for h in range(heads):
        slide(h, 1, steps, bias)

    qt[...] = qf[...].astype(F32).T
    entering = jnp.exp(crow[...])
    for h in range(heads):
        phiq[h] = fold_features(
            qt[h * width:(h + 1) * width, :], entering[h:h + 1, :], 1.0 / 32, 1.0 / 16, 0.25)

    if groups > 1:
        for c in range(per):
            pass_on(c)

    @pl.when(me > 0)
    def _():
        halo_copy(1).wait_recv()
        halo_copy(2).wait_recv()

    first_bias = jnp.where(band & ((col >= WINDOW) | (me > 0)), 0.0, -1e30)
    for h in range(heads):
        slide(h, 0, 1, first_bias)

    pick_a = jnp.where(slab_row == NORM_A, 1.0, 0.0).astype(BF16)
    pick_b = jnp.where(slab_row == NORM_B, 1.0, 0.0).astype(BF16)
    for c in range(per):
        for h in range(c * group, (c + 1) * group):
            @pl.when((h % group != r) & (me > 0))
            def _(h=h):
                e_arrival(h).wait_recv()

        for h in range(c * group, (c + 1) * group):
            lanes = slice(h * size, (h + 1) * size)
            before = e_recv[h]
            slab = before[SLAB:SLAB + 16, :]
            norm = jnp.concatenate(
                [dot_first(slab, pick_a), dot_first(slab, pick_b)[0:FOLDED - SLAB]], axis=0).astype(BF16)
            both = numden[h] + dot_first(phiq[h], jnp.concatenate([before, norm], axis=1))
            out[:, lanes] = (both[:, 0:size] / both[:, size:2 * size] + win[:, lanes]).astype(BF16)

    @pl.when(me < n - 1)
    def _():
        for which in range(3):
            halo_copy(which).wait_send()

    for h in range(heads):
        @pl.when((r != h % group) & (me < n - 1))
        def _(h=h):
            s_copy(h).wait_send()

    for c in range(per):
        for target in range(1, groups):
            @pl.when(target > g)
            def _(target=target, c=c):
                t_copy(c, target).wait_send()

        for target in range(group):
            @pl.when((target != r) & ((g > 0) | (target > 0)))
            def _(target=target, c=c):
                e_copy(c, target).wait_send()


def solution(mesh):
    n = mesh.shape["seq"]

    def local(q_feat, k_feat, values, win_query, win_key, log_gates, conv_weight):
        tok, channels = values.shape
        heads = log_gates.shape[1]
        size = channels // heads
        width = q_feat.shape[1] // heads
        group = next(s for s in (4, 2, 1) if n % s == 0 and heads % s == 0)
        groups, per = n // group, heads // group
        hbm = pl.BlockSpec(memory_space=pltpu.HBM)
        dma = pltpu.SemaphoreType.DMA
        block = (FOLDED, size)
        operands = (q_feat, k_feat, log_gates.T, conv_weight, values, win_key, win_query)
        return pl.pallas_call(
            functools.partial(kernel, n, group, heads, size, width),
            out_shape=jax.ShapeDtypeStruct((tok, channels), BF16),
            in_specs=[hbm] * 7,
            out_specs=pl.BlockSpec(memory_space=pltpu.VMEM),
            scratch_shapes=[
                pltpu.VMEM(q_feat.shape, BF16),
                pltpu.VMEM(k_feat.shape, BF16),
                pltpu.VMEM((heads, tok), F32),
                pltpu.VMEM(conv_weight.shape, F32),
                pltpu.VMEM((tok + WINDOW, channels), BF16),
                pltpu.VMEM((tok + WINDOW, channels), BF16),
                pltpu.VMEM((tok, channels), BF16),
                pltpu.VMEM((16, channels), BF16),
                pltpu.VMEM((tok + 8, channels), F32),
                pltpu.VMEM((heads, tok, 2 * size), BF16),
                pltpu.VMEM((heads * width, tok), F32),
                pltpu.VMEM((heads * width, tok), F32),
                pltpu.VMEM((heads, FOLDED, tok), BF16),
                pltpu.VMEM((heads, FOLDED, tok), BF16),
                pltpu.VMEM((heads, tok, 2 * size), F32),
                pltpu.VMEM((tok, channels), F32),
                pltpu.VMEM((tok, 128), F32),
                pltpu.VMEM((heads, tok), F32),
                pltpu.VMEM((heads,) + block, F32),
                pltpu.VMEM((heads,) + block, BF16),
                pltpu.VMEM((per, group) + block, BF16),
                pltpu.VMEM((per, group) + block, F32),
                pltpu.VMEM((heads, 1, size), F32),
                pltpu.VMEM(block, F32),
                pltpu.VMEM((per,) + block, BF16),
                pltpu.VMEM((per, groups) + block, BF16),
                pltpu.VMEM((per, group) + block, BF16),
                pltpu.VMEM((heads,) + block, BF16),
                dma((7,)), dma((3,)), dma((3,)),
                dma((heads,)), dma((per, group)), dma((per, groups)), dma((per, groups)),
                dma((per, group)), dma((heads,)),
            ],
            compiler_params=pltpu.CompilerParams(
                collective_id=0, has_side_effects=True, vmem_limit_bytes=40 * 1024 * 1024),
        )(*[pltpu.with_memory_space_constraint(x, pltpu.HBM) for x in operands])

    shard = P(("grp", "seq"), "head")
    return jax.shard_map(
        local, mesh=mesh, in_specs=(shard,) * 6 + (P(None, "head"),), out_specs=shard, check_vma=False)
```

```python
import functools

import jax
import jax.numpy as jnp
from jax import lax
from jax.experimental import pallas as pl
from jax.experimental.pallas import tpu as pltpu
from jax.sharding import PartitionSpec as P

WINDOW = 64
TILE = 128
FOLDED = 160
SLAB = 128
NORM, KEY_0, KEY_1, MIX, LAST_2, LAST_1 = 9, 10, 11, 12, 13, 14
REST = FOLDED - SLAB
FADE_HI, FADE_LO = 96, 112
EARLY = 4
PIECE = 16
F32 = jnp.float32
BF16 = jnp.bfloat16
MESH = pl.DeviceIdType.MESH


def dot(a, b):
    return lax.dot_general(a, b, (((1,), (0,)), ((), ())), preferred_element_type=F32)


def dot_t(a, b):
    return lax.dot_general(a, b, (((1,), (1,)), ((), ())), preferred_element_type=F32)


def dot_first(a, b):
    return lax.dot_general(a, b, (((0,), (0,)), ((), ())), preferred_element_type=F32)


def fold_features(x, level, square_scale, pair_scale, linear_scale):
    rows = lax.broadcasted_iota(jnp.int32, x.shape, 0)
    levelled = x * level
    scaled = levelled * pair_scale
    parts = [(levelled * square_scale) * x]
    for step in range(1, 8):
        parts.append(scaled * pltpu.roll(x, 16 - step, 0))
    half = scaled * pltpu.roll(x, 8, 0)
    parts.append(jnp.where(rows < 8, half, jnp.where(rows == 8, level, 0.0)))
    parts.append(levelled * linear_scale)
    return jnp.concatenate([part.astype(BF16) for part in parts], axis=0)


def kernel(
    n, group, heads, size, width,
    q_feat, k_feat, log_gates, conv_weight, values, win_key, win_query,
    out,
    qf, kf, gates, weight,
    vx, kx, wq, vf, vw, qt, kt, phik, phiq, numden, win, ccol, crow,
    s_send, s_recv, e_group, faded, before_group, t_send, t_recv, e_send, e_recv,
    in_sem, halo_send, halo_recv, ss_sem, sr_sem, ts_sem, tr_sem, es_sem, er_sem,
):
    me = lax.axis_index("seq")
    groups = n // group
    per = heads // group
    g = me // group
    r = lax.rem(me, group)
    tok = qf.shape[0]
    tiles = tok // TILE
    tail = WINDOW
    pieces = tail // PIECE

    loads = [
        pltpu.make_async_copy(log_gates, gates, in_sem.at[0]),
        pltpu.make_async_copy(k_feat, kf, in_sem.at[1]),
        pltpu.make_async_copy(values, vx.at[pl.ds(tail, tok)], in_sem.at[2]),
        pltpu.make_async_copy(conv_weight, weight, in_sem.at[3]),
        pltpu.make_async_copy(q_feat, qf, in_sem.at[4]),
        pltpu.make_async_copy(win_key, kx.at[pl.ds(tail, tok)], in_sem.at[5]),
        pltpu.make_async_copy(win_query, wq, in_sem.at[6]),
    ]
    for load in loads:
        load.start()
    load_g, load_kf, load_v, load_w, load_qf, load_k, load_q = loads

    barrier = pltpu.get_barrier_semaphore()

    def greet(peer):
        pl.semaphore_signal(barrier, inc=1, device_id={"seq": peer}, device_id_type=MESH)

    for turn in range(1, group):
        greet(g * group + lax.rem(r + turn, group))
    for turn in range(1, groups):
        greet(lax.rem(me + turn * group, n))
    across_next = (r == group - 1) & (g < groups - 1)
    across_prev = (r == 0) & (g > 0)

    @pl.when(across_next)
    def _():
        greet(me + 1)

    @pl.when(across_prev)
    def _():
        greet(me - 1)

    @pl.when(me == 0)
    def _():
        vx[0:tail, :] = jnp.zeros((tail, heads * size), BF16)
        kx[0:tail, :] = jnp.zeros((tail, heads * size), BF16)

    vf[0:8, :] = jnp.zeros((8, heads * size), F32)
    nxt = lax.rem(me + 1, n)

    def halo_copy(which):
        source, target = ((values, vx), (win_key, kx))[which // pieces]
        start = tail - PIECE * (which % pieces + 1)
        return pltpu.make_async_remote_copy(
            source.at[pl.ds(tok - tail + start, PIECE)], target.at[pl.ds(start, PIECE)],
            halo_send.at[which], halo_recv.at[which], device_id={"seq": nxt}, device_id_type=MESH)

    def send_halo(*which):
        @pl.when(me < n - 1)
        def _():
            for piece in which:
                halo_copy(piece).start()

    def turned(turn):
        return lax.rem(r + turn, group)

    def s_copy(c, owner):
        return pltpu.make_async_remote_copy(
            s_send.at[c * group + owner], s_recv.at[c, r], ss_sem.at[c * group + owner], sr_sem.at[c, r],
            device_id={"seq": g * group + owner}, device_id_type=MESH)

    def s_arrival(c, source):
        return pltpu.make_async_remote_copy(
            s_send.at[c * group], s_recv.at[c, source], ss_sem.at[c * group], sr_sem.at[c, source],
            device_id={"seq": g * group + source}, device_id_type=MESH)

    def t_copy(c, target):
        return pltpu.make_async_remote_copy(
            t_send.at[c], t_recv.at[c, g], ts_sem.at[c, target], tr_sem.at[c, g],
            device_id={"seq": target * group + r}, device_id_type=MESH)

    def t_arrival(c, source):
        return pltpu.make_async_remote_copy(
            t_send.at[c], t_recv.at[c, source], ts_sem.at[c, source], tr_sem.at[c, source],
            device_id={"seq": source * group + r}, device_id_type=MESH)

    def e_copy(c, target):
        return pltpu.make_async_remote_copy(
            e_send.at[c, target], e_recv.at[c * group + r], es_sem.at[c, target], er_sem.at[c * group + r],
            device_id={"seq": g * group + target}, device_id_type=MESH)

    def e_arrival(h):
        return pltpu.make_async_remote_copy(
            e_send.at[0, 0], e_recv.at[h], es_sem.at[0, 0], er_sem.at[h],
            device_id={"seq": g * group + lax.rem(h, group)}, device_id_type=MESH)

    before_or_at = jnp.where(
        lax.broadcasted_iota(jnp.int32, (tok, tok), 0) <= lax.broadcasted_iota(jnp.int32, (tok, tok), 1),
        1.0, 0.0).astype(BF16)
    load_g.wait()
    upper = gates[...].astype(BF16)
    rest = gates[...] - upper.astype(F32)
    middle = rest.astype(BF16)
    lowest = (rest - middle.astype(F32)).astype(BF16)
    total = dot(jnp.concatenate([upper, middle, lowest], axis=0), before_or_at)
    total = total[0:heads] + (total[heads:2 * heads] + total[2 * heads:3 * heads])
    crow[...] = total
    ccol[...] = jnp.concatenate([total, jnp.zeros((128 - heads, tok), F32)], axis=0).T
    keep_row = jnp.exp(total[:, tok - 1:tok] - total)
    finish = jnp.exp(total[:, tok - 1:tok])
    finish_hi = finish.astype(BF16).astype(F32)
    finish_lo = finish - finish_hi

    load_kf.wait()
    kt[...] = kf[...].astype(F32).T
    for h in range(heads):
        phik[h] = fold_features(
            kt[h * width:(h + 1) * width, :], keep_row[h:h + 1, :], 1.0, 1.0, 1.0)

    load_w.wait()
    load_v.wait()
    slab_row = lax.broadcasted_iota(jnp.int32, (16, size), 0)
    slab_lane = lax.broadcasted_iota(jnp.int32, (16, size), 1)
    probe_row = lax.broadcasted_iota(jnp.int32, (16, tok), 0)
    probe_lane = lax.broadcasted_iota(jnp.int32, (16, tok), 1)
    probes = jnp.where((probe_row == 0) | (probe_lane == probe_row - 1), 1.0, 0.0).astype(BF16)
    late = (r == 0) & (g > 0)

    def state(h):
        lanes = slice(h * size, (h + 1) * size)
        current = vx[tail:tail + tok, lanes].astype(F32)
        vf[8:8 + tok, lanes] = current
        conv = weight[0:1, lanes] * current
        for tap in range(1, weight.shape[0]):
            conv = conv + weight[tap:tap + 1, lanes] * vf[8 - tap:8 - tap + tok, lanes]
        conv = conv.astype(BF16)
        vw[h, :, 0:size] = conv
        vw[h, :, size:2 * size] = jnp.ones((tok, size), BF16)
        folded = dot(phik[h], conv)
        probed = dot_t(probes, phik[h])
        ends = jnp.concatenate([probed[:, SLAB:FOLDED], jnp.zeros((16, SLAB - REST), F32)], axis=1)
        mix = (ends[0:1, :] + pltpu.roll(ends, REST, 1)[1:2, :] + pltpu.roll(ends, 2 * REST, 1)[2:3, :])
        mix = jnp.where(slab_lane[0:1, :] >= FADE_HI, finish_hi[h:h + 1, :], mix)
        mix = jnp.where(slab_lane[0:1, :] >= FADE_LO, finish_lo[h:h + 1, :], mix)
        slab = folded[SLAB:SLAB + 16, :]
        for at, line in ((NORM, probed[0:1, 0:SLAB]), (KEY_0, probed[1:2, 0:SLAB]), (KEY_1, probed[2:3, 0:SLAB]),
                         (MIX, mix), (LAST_2, current[tok - 2:tok - 1, :]), (LAST_1, current[tok - 1:tok, :])):
            slab = jnp.where(slab_row == at, line, slab)
        s_send[h] = jnp.concatenate([folded[0:SLAB, :], slab, folded[SLAB + 16:, :]], axis=0).astype(BF16)

    def send_states(c):
        for turn in range(1, group):
            s_copy(c, turned(turn)).start()

    def correct(h, first):
        lanes = slice(h * size, (h + 1) * size)
        change = first[:, lanes].astype(F32) - vw[h, 0:16, 0:size].astype(F32)
        vw[h, 0:16, 0:size] = first[:, lanes]
        return change

    def first_rows():
        halo_copy(0).wait_recv()
        vf[0:8, :] = vx[tail - 16:tail, :].astype(F32)[8:16, :]
        first = weight[0:1, :] * vf[8:24, :]
        for tap in range(1, weight.shape[0]):
            first = first + weight[tap:tap + 1, :] * vf[8 - tap:24 - tap, :]
        return first.astype(BF16)

    for h in range(EARLY):
        state(h)
    pl.semaphore_wait(
        barrier, (group - 1) + (groups - 1) + across_next.astype(jnp.int32) + across_prev.astype(jnp.int32))

    send_halo(0)

    for c in range(per):
        for h in range(c * group, (c + 1) * group):
            if h >= EARLY:
                state(h)

        @pl.when(jnp.logical_not(late))
        def _(c=c):
            send_states(c)

    @pl.when(late)
    def _():
        first = first_rows()
        for h in range(heads):
            change = jnp.concatenate(
                [correct(h, first).astype(BF16), jnp.zeros((TILE - 16, size), BF16)], axis=0)
            s_send[h] = (s_send[h].astype(F32) + dot(phik[h, :, 0:TILE], change)).astype(BF16)
        for c in range(per):
            send_states(c)

    for c in range(per):
        s_recv[c, r] = s_send[c * group + r]

    lane_head = lax.broadcasted_iota(jnp.int32, (tok, heads * width), 1) // width
    load_qf.wait()
    kt_narrow = kt[...].astype(BF16)
    q_quarter = qf[...] * jnp.asarray(0.25, BF16)
    diagonal = (lax.broadcasted_iota(jnp.int32, (TILE, TILE), 0)
                >= lax.broadcasted_iota(jnp.int32, (TILE, TILE), 1))

    def scores(h):
        lone = jnp.where(lane_head == h, q_quarter, jnp.zeros_like(q_quarter))
        for i in range(tiles):
            t0 = i * TILE
            reach = t0 + TILE
            x = dot(lone[t0:reach, :], kt_narrow[:, 0:reach])
            poly = 1.0 + x * (1.0 + 0.5 * x)
            gap = ccol[t0:reach, h:h + 1] - crow[h:h + 1, 0:reach]
            last = jnp.where(diagonal, gap[:, t0:reach], -1e30)
            if i > 0:
                gap = jnp.concatenate([gap[:, 0:t0], last], axis=1)
            else:
                gap = last
            score = (poly * jnp.exp(gap)).astype(BF16)
            numden[h, t0:reach, :] = dot(score, vw[h, 0:reach, :])

    def fade_of(slab):
        return slab[MIX:MIX + 1, FADE_HI:FADE_HI + 1] + slab[MIX:MIX + 1, FADE_LO:FADE_LO + 1]

    def across(c, slab, last_slab):
        lanes = pl.ds(pl.multiple_of((c * group + r) * size, size), size)
        taps = weight[:, lanes]
        last = last_slab.astype(F32)
        last_1, last_2 = last[LAST_1:LAST_1 + 1, :], last[LAST_2:LAST_2 + 1, :]
        change_0 = taps[1:2, :] * last_1 + taps[2:3, :] * last_2
        change_1 = taps[2:3, :] * last_1
        at_a = jnp.where(slab_row == KEY_0, change_0, jnp.where(slab_row == KEY_1, change_1, 0.0))
        at_0 = jnp.where(slab_row == MIX, change_0, 0.0)
        at_1 = jnp.where(slab_row == MIX, change_1, 0.0)
        out = dot_first(slab, jnp.concatenate([at_a, at_0, at_1], axis=1).astype(BF16))
        rest = out[REST:2 * REST, size:2 * size] + out[2 * REST:3 * REST, 2 * size:3 * size]
        return jnp.concatenate([out[:, 0:size], rest], axis=0)

    def emit(c, earlier):
        def entering(i):
            e = e_group[c, i]
            return (e if earlier is None else e + faded[c * group + i] * earlier).astype(BF16)

        for turn in range(1, group):
            target = turned(turn)
            e_send[c, target] = entering(target)
            e_copy(c, target).start()
        e_recv[c * group + r] = entering(r)

    def gather(c):
        for turn in range(1, group):
            s_arrival(c, turned(turn)).wait_recv()
        running = jnp.zeros((FOLDED, size), F32)
        fades = jnp.ones((1, size), F32)

        def step(j, running, fades):
            block = s_recv[c, j].astype(F32)
            fade = fade_of(block[SLAB:SLAB + 16, :])
            running = fade * running + block
            if j > 0:
                running = running + across(
                    c, s_recv[c, j, SLAB:SLAB + 16, :], s_recv[c, j - 1, SLAB:SLAB + 16, :])
            return running, fades * fade

        for j in range(group - 1):
            e_group[c, j] = running
            faded[c * group + j] = fades
            running, fades = step(j, running, fades)
        e_group[c, group - 1] = running
        faded[c * group + group - 1] = fades

        @pl.when(g < groups - 1)
        def _():
            total, whole = step(group - 1, running, fades)
            whole_hi = whole.astype(BF16).astype(F32)
            slab = total[SLAB:SLAB + 16, :]
            slab = jnp.where((slab_row == MIX) & (slab_lane >= FADE_HI), whole_hi, slab)
            slab = jnp.where((slab_row == MIX) & (slab_lane >= FADE_LO), whole - whole_hi, slab)
            t_send[c] = jnp.concatenate(
                [total[0:SLAB, :], slab, total[SLAB + 16:, :]], axis=0).astype(BF16)
            for target in range(1, groups):
                @pl.when(target > g)
                def _(target=target):
                    t_copy(c, target).start()

        @pl.when(g == 0)
        def _():
            emit(c, None)

    def pass_on(c):
        @pl.when(g > 0)
        def _():
            t_arrival(c, 0).wait_recv()
            before_group[...] = t_recv[c, 0].astype(F32)
            for source in range(1, groups - 1):
                @pl.when(source < g)
                def _(source=source):
                    t_arrival(c, source).wait_recv()
                    block = t_recv[c, source].astype(F32)
                    before_group[...] = fade_of(block[SLAB:SLAB + 16, :]) * before_group[...] + block
            emit(c, before_group[...])

    row = lax.broadcasted_iota(jnp.int32, (WINDOW, 2 * WINDOW), 0)
    col = lax.broadcasted_iota(jnp.int32, (WINDOW, 2 * WINDOW), 1)
    band = (col > row) & (col <= row + WINDOW)
    steps = tok // WINDOW
    scale = size ** (-0.5)
    ones = jnp.ones((2 * WINDOW, size), BF16)

    def slide(h, start, stop, bias):
        lanes = slice(h * size, (h + 1) * size)
        s = jnp.concatenate([
            dot_t(wq[i * WINDOW:(i + 1) * WINDOW, lanes], kx[i * WINDOW:(i + 2) * WINDOW, lanes])
            for i in range(start, stop)], axis=0)
        s = s * scale + bias
        p = jnp.exp(s - jnp.max(s, axis=1, keepdims=True)).astype(BF16)
        pv = jnp.concatenate([
            dot(p[(i - start) * WINDOW:(i - start + 1) * WINDOW, :],
                jnp.concatenate([vx[i * WINDOW:(i + 2) * WINDOW, lanes], ones], axis=1))
            for i in range(start, stop)], axis=0)
        win[start * WINDOW:stop * WINDOW, lanes] = pv[:, 0:size] / pv[:, size:2 * size]

    load_k.wait()
    load_q.wait()
    bias = jnp.concatenate([jnp.where(band, 0.0, -1e30)] * (steps - 1), axis=0)
    for h in range(0, 4):
        slide(h, 1, steps, bias)

    send_halo(1)

    for h in range(4, 8):
        slide(h, 1, steps, bias)

    send_halo(2)

    @pl.when((me > 0) & jnp.logical_not(late))
    def _():
        first = first_rows()
        for h in range(heads):
            correct(h, first)

    for h in range(0, 1):
        scores(h)

    send_halo(3)

    for h in range(1, 2):
        scores(h)

    send_halo(4)

    for h in range(2, 3):
        scores(h)

    send_halo(5)

    for h in range(3, 4):
        scores(h)

    send_halo(6)

    for h in range(4, 5):
        scores(h)

    send_halo(7)

    gather(0)

    for h in range(5, 6):
        scores(h)

    gather(1)

    for h in range(6, 8):
        scores(h)

    pass_on(0)

    pass_on(1)

    qt[...] = qf[...].astype(F32).T
    entering = jnp.exp(crow[...])
    for h in range(heads):
        phiq[h] = fold_features(
            qt[h * width:(h + 1) * width, :], entering[h:h + 1, :], 1.0 / 32, 1.0 / 16, 0.25).T

    @pl.when(me > 0)
    def _():
        for which in range(1, 2 * pieces):
            halo_copy(which).wait_recv()

    first_bias = jnp.where(band & ((col >= WINDOW) | (me > 0)), 0.0, -1e30)
    for h in range(heads):
        slide(h, 0, 1, first_bias)

    picks = jnp.concatenate(
        [jnp.where(slab_row == at, 1.0, 0.0) for at in (NORM, MIX)], axis=1).astype(BF16)
    for c in range(per):
        for turn in range(1, group):
            e_arrival(c * group + turned(turn)).wait_recv()

        for h in range(c * group, (c + 1) * group):
            lanes = slice(h * size, (h + 1) * size)
            before = e_recv[h]
            norm = dot_first(before[SLAB:SLAB + 16, :], picks)
            norm = jnp.concatenate([norm[:, 0:size], norm[0:REST, size:2 * size]], axis=0).astype(BF16)
            both = numden[h] + dot(phiq[h], jnp.concatenate([before, norm], axis=1))
            out[:, lanes] = (both[:, 0:size] / both[:, size:2 * size] + win[:, lanes]).astype(BF16)

    @pl.when(me < n - 1)
    def _():
        for which in range(2 * pieces):
            halo_copy(which).wait_send()

    for c in range(per):
        for turn in range(1, group):
            s_copy(c, turned(turn)).wait_send()
            e_copy(c, turned(turn)).wait_send()

        for target in range(1, groups):
            @pl.when(target > g)
            def _(target=target, c=c):
                t_copy(c, target).wait_send()


def solution(mesh):
    n = mesh.shape["seq"]

    def local(q_feat, k_feat, values, win_query, win_key, log_gates, conv_weight):
        tok, channels = values.shape
        heads = log_gates.shape[1]
        size = channels // heads
        width = q_feat.shape[1] // heads
        group = next(s for s in (4, 2, 1) if n % s == 0 and heads % s == 0)
        groups, per = n // group, heads // group
        hbm = pl.BlockSpec(memory_space=pltpu.HBM)
        dma = pltpu.SemaphoreType.DMA
        block = (FOLDED, size)
        operands = (q_feat, k_feat, log_gates.T, conv_weight, values, win_key, win_query)
        return pl.pallas_call(
            functools.partial(kernel, n, group, heads, size, width),
            out_shape=jax.ShapeDtypeStruct((tok, channels), BF16),
            in_specs=[hbm] * 7,
            out_specs=pl.BlockSpec(memory_space=pltpu.VMEM),
            scratch_shapes=[
                pltpu.VMEM(q_feat.shape, BF16),
                pltpu.VMEM(k_feat.shape, BF16),
                pltpu.VMEM((heads, tok), F32),
                pltpu.VMEM(conv_weight.shape, F32),
                pltpu.VMEM((tok + WINDOW, channels), BF16),
                pltpu.VMEM((tok + WINDOW, channels), BF16),
                pltpu.VMEM((tok, channels), BF16),
                pltpu.VMEM((tok + 8, channels), F32),
                pltpu.VMEM((heads, tok, 2 * size), BF16),
                pltpu.VMEM((heads * width, tok), F32),
                pltpu.VMEM((heads * width, tok), F32),
                pltpu.VMEM((heads, FOLDED, tok), BF16),
                pltpu.VMEM((heads, tok, FOLDED), BF16),
                pltpu.VMEM((heads, tok, 2 * size), F32),
                pltpu.VMEM((tok, channels), F32),
                pltpu.VMEM((tok, 128), F32),
                pltpu.VMEM((heads, tok), F32),
                pltpu.VMEM((heads,) + block, BF16),
                pltpu.VMEM((per, group) + block, BF16),
                pltpu.VMEM((per, group) + block, F32),
                pltpu.VMEM((heads, 1, size), F32),
                pltpu.VMEM(block, F32),
                pltpu.VMEM((per,) + block, BF16),
                pltpu.VMEM((per, groups) + block, BF16),
                pltpu.VMEM((per, group) + block, BF16),
                pltpu.VMEM((heads,) + block, BF16),
                dma((7,)), dma((2 * WINDOW // PIECE,)), dma((2 * WINDOW // PIECE,)),
                dma((heads,)), dma((per, group)), dma((per, groups)), dma((per, groups)),
                dma((per, group)), dma((heads,)),
            ],
            compiler_params=pltpu.CompilerParams(
                collective_id=0, has_side_effects=True, vmem_limit_bytes=40 * 1024 * 1024),
        )(*[pltpu.with_memory_space_constraint(x, pltpu.HBM) for x in operands])

    shard = P(("grp", "seq"), "head")
    return jax.shard_map(
        local, mesh=mesh, in_specs=(shard,) * 6 + (P(None, "head"),), out_specs=shard, check_vma=False)
```

```python
import functools

import jax
import jax.numpy as jnp
from jax import lax
from jax.experimental import pallas as pl
from jax.experimental.pallas import tpu as pltpu
from jax.sharding import PartitionSpec as P

WINDOW = 64
TILE = 128
FOLDED = 160
SLAB = 128
NORM, KEY_0, KEY_1, MIX, LAST_2, LAST_1 = 9, 10, 11, 12, 13, 14
REST = FOLDED - SLAB
FADE_HI, FADE_LO = 96, 112
EARLY = 4
PIECE = 16
F32 = jnp.float32
BF16 = jnp.bfloat16
MESH = pl.DeviceIdType.MESH


def dot(a, b):
    return lax.dot_general(a, b, (((1,), (0,)), ((), ())), preferred_element_type=F32)


def dot_t(a, b):
    return lax.dot_general(a, b, (((1,), (1,)), ((), ())), preferred_element_type=F32)


def dot_first(a, b):
    return lax.dot_general(a, b, (((0,), (0,)), ((), ())), preferred_element_type=F32)


def inverse(x):
    guess = pl.reciprocal(x, approx=True)
    return guess * (2.0 - x * guess)


def fold_features(x, level, square_scale, pair_scale, linear_scale):
    rows = lax.broadcasted_iota(jnp.int32, x.shape, 0)
    levelled = x * level
    scaled = levelled * pair_scale
    parts = [(levelled * square_scale) * x]
    for step in range(1, 8):
        parts.append(scaled * pltpu.roll(x, 16 - step, 0))
    half = scaled * pltpu.roll(x, 8, 0)
    parts.append(jnp.where(rows < 8, half, jnp.where(rows == 8, level, 0.0)))
    parts.append(levelled * linear_scale)
    return jnp.concatenate([part.astype(BF16) for part in parts], axis=0)


def kernel(
    n, group, heads, size, width,
    q_feat, k_feat, log_gates, conv_weight, values, win_key, win_query,
    out,
    qf, kf, gates, weight,
    vx, kx, wq, vf, vw, qt, kt, phik, phiq, numden, win, ccol, crow,
    s_send, s_recv, e_group, faded, before_group, t_send, t_recv, e_send, e_recv,
    in_sem, halo_send, halo_recv, ss_sem, sr_sem, ts_sem, tr_sem, es_sem, er_sem,
):
    me = lax.axis_index("seq")
    groups = n // group
    per = heads // group
    g = me // group
    r = lax.rem(me, group)
    tok = qf.shape[0]
    tiles = tok // TILE
    tail = WINDOW
    pieces = tail // PIECE

    loads = [
        pltpu.make_async_copy(log_gates, gates, in_sem.at[0]),
        pltpu.make_async_copy(k_feat, kf, in_sem.at[1]),
        pltpu.make_async_copy(values, vx.at[pl.ds(tail, tok)], in_sem.at[2]),
        pltpu.make_async_copy(conv_weight, weight, in_sem.at[3]),
        pltpu.make_async_copy(q_feat, qf, in_sem.at[4]),
        pltpu.make_async_copy(win_key, kx.at[pl.ds(tail, tok)], in_sem.at[5]),
        pltpu.make_async_copy(win_query, wq, in_sem.at[6]),
    ]
    for load in loads[:5]:
        load.start()
    load_g, load_kf, load_v, load_w, load_qf, load_k, load_q = loads

    barrier = pltpu.get_barrier_semaphore()

    def greet(peer):
        pl.semaphore_signal(barrier, inc=1, device_id={"seq": peer}, device_id_type=MESH)

    for turn in range(1, group):
        greet(g * group + lax.rem(r + turn, group))
    for turn in range(1, groups):
        greet(lax.rem(me + turn * group, n))
    across_next = (r == group - 1) & (g < groups - 1)
    across_prev = (r == 0) & (g > 0)

    @pl.when(across_next)
    def _():
        greet(me + 1)

    @pl.when(across_prev)
    def _():
        greet(me - 1)

    @pl.when(me == 0)
    def _():
        vx[0:tail, :] = jnp.zeros((tail, heads * size), BF16)
        kx[0:tail, :] = jnp.zeros((tail, heads * size), BF16)

    vf[0:8, :] = jnp.zeros((8, heads * size), F32)
    nxt = lax.rem(me + 1, n)

    def halo_copy(which):
        source, target = ((values, vx), (win_key, kx))[which // pieces]
        start = tail - PIECE * (which % pieces + 1)
        return pltpu.make_async_remote_copy(
            source.at[pl.ds(tok - tail + start, PIECE)], target.at[pl.ds(start, PIECE)],
            halo_send.at[which], halo_recv.at[which], device_id={"seq": nxt}, device_id_type=MESH)

    def send_halo(*which):
        @pl.when(me < n - 1)
        def _():
            for piece in which:
                halo_copy(piece).start()

    def turned(turn):
        return lax.rem(r + turn, group)

    def s_copy(c, owner):
        return pltpu.make_async_remote_copy(
            s_send.at[c * group + owner], s_recv.at[c, r], ss_sem.at[c * group + owner], sr_sem.at[c, r],
            device_id={"seq": g * group + owner}, device_id_type=MESH)

    def s_arrival(c, source):
        return pltpu.make_async_remote_copy(
            s_send.at[c * group], s_recv.at[c, source], ss_sem.at[c * group], sr_sem.at[c, source],
            device_id={"seq": g * group + source}, device_id_type=MESH)

    def t_copy(c, target):
        return pltpu.make_async_remote_copy(
            t_send.at[c], t_recv.at[c, g], ts_sem.at[c, target], tr_sem.at[c, g],
            device_id={"seq": target * group + r}, device_id_type=MESH)

    def t_arrival(c, source):
        return pltpu.make_async_remote_copy(
            t_send.at[c], t_recv.at[c, source], ts_sem.at[c, source], tr_sem.at[c, source],
            device_id={"seq": source * group + r}, device_id_type=MESH)

    def e_copy(c, target):
        return pltpu.make_async_remote_copy(
            e_send.at[c, target], e_recv.at[c * group + r], es_sem.at[c, target], er_sem.at[c * group + r],
            device_id={"seq": g * group + target}, device_id_type=MESH)

    def e_arrival(h):
        return pltpu.make_async_remote_copy(
            e_send.at[0, 0], e_recv.at[h], es_sem.at[0, 0], er_sem.at[h],
            device_id={"seq": g * group + lax.rem(h, group)}, device_id_type=MESH)

    before_or_at = jnp.where(
        lax.broadcasted_iota(jnp.int32, (tok, tok), 0) <= lax.broadcasted_iota(jnp.int32, (tok, tok), 1),
        1.0, 0.0).astype(BF16)
    load_g.wait()
    upper = gates[...].astype(BF16)
    rest = gates[...] - upper.astype(F32)
    middle = rest.astype(BF16)
    lowest = (rest - middle.astype(F32)).astype(BF16)
    total = dot(jnp.concatenate([upper, middle, lowest], axis=0), before_or_at)
    total = total[0:heads] + (total[heads:2 * heads] + total[2 * heads:3 * heads])
    crow[...] = total
    ccol[...] = jnp.concatenate([total, jnp.zeros((128 - heads, tok), F32)], axis=0).T
    keep_row = jnp.exp(total[:, tok - 1:tok] - total)
    finish = jnp.exp(total[:, tok - 1:tok])
    finish_hi = finish.astype(BF16).astype(F32)
    finish_lo = finish - finish_hi

    load_kf.wait()
    kt[...] = kf[...].astype(F32).T
    for h in range(heads):
        phik[h] = fold_features(
            kt[h * width:(h + 1) * width, :], keep_row[h:h + 1, :], 1.0, 1.0, 1.0)

    load_w.wait()
    load_v.wait()
    loads[5].start()
    loads[6].start()
    slab_row = lax.broadcasted_iota(jnp.int32, (16, size), 0)
    slab_lane = lax.broadcasted_iota(jnp.int32, (16, size), 1)
    probe_row = lax.broadcasted_iota(jnp.int32, (16, tok), 0)
    probe_lane = lax.broadcasted_iota(jnp.int32, (16, tok), 1)
    probes = jnp.where((probe_row == 0) | (probe_lane == probe_row - 1), 1.0, 0.0).astype(BF16)
    late = (r == 0) & (g > 0)

    def state(h):
        lanes = slice(h * size, (h + 1) * size)
        current = vx[tail:tail + tok, lanes].astype(F32)
        vf[8:8 + tok, lanes] = current
        conv = weight[0:1, lanes] * current
        for tap in range(1, weight.shape[0]):
            conv = conv + weight[tap:tap + 1, lanes] * vf[8 - tap:8 - tap + tok, lanes]
        conv = conv.astype(BF16)
        vw[h, :, 0:size] = conv
        vw[h, :, size:2 * size] = jnp.ones((tok, size), BF16)
        folded = dot(phik[h], conv)
        probed = dot_t(probes, phik[h])
        ends = jnp.concatenate([probed[:, SLAB:FOLDED], jnp.zeros((16, SLAB - REST), F32)], axis=1)
        mix = (ends[0:1, :] + pltpu.roll(ends, REST, 1)[1:2, :] + pltpu.roll(ends, 2 * REST, 1)[2:3, :])
        mix = jnp.where(slab_lane[0:1, :] >= FADE_HI, finish_hi[h:h + 1, :], mix)
        mix = jnp.where(slab_lane[0:1, :] >= FADE_LO, finish_lo[h:h + 1, :], mix)
        slab = folded[SLAB:SLAB + 16, :]
        for at, line in ((NORM, probed[0:1, 0:SLAB]), (KEY_0, probed[1:2, 0:SLAB]), (KEY_1, probed[2:3, 0:SLAB]),
                         (MIX, mix), (LAST_2, current[tok - 2:tok - 1, :]), (LAST_1, current[tok - 1:tok, :])):
            slab = jnp.where(slab_row == at, line, slab)
        s_send[h] = jnp.concatenate([folded[0:SLAB, :], slab, folded[SLAB + 16:, :]], axis=0).astype(BF16)

    def send_states(c):
        for turn in range(1, group):
            s_copy(c, turned(turn)).start()

    def correct(h, first):
        lanes = slice(h * size, (h + 1) * size)
        change = first[:, lanes].astype(F32) - vw[h, 0:16, 0:size].astype(F32)
        vw[h, 0:16, 0:size] = first[:, lanes]
        return change

    def first_rows():
        halo_copy(0).wait_recv()
        vf[0:8, :] = vx[tail - 16:tail, :].astype(F32)[8:16, :]
        first = weight[0:1, :] * vf[8:24, :]
        for tap in range(1, weight.shape[0]):
            first = first + weight[tap:tap + 1, :] * vf[8 - tap:24 - tap, :]
        return first.astype(BF16)

    for h in range(EARLY):
        state(h)
    pl.semaphore_wait(
        barrier, (group - 1) + (groups - 1) + across_next.astype(jnp.int32) + across_prev.astype(jnp.int32))

    send_halo(0)

    for c in range(per):
        for h in range(c * group, (c + 1) * group):
            if h >= EARLY:
                state(h)

        @pl.when(jnp.logical_not(late))
        def _(c=c):
            send_states(c)

    @pl.when(late)
    def _():
        first = first_rows()
        for h in range(heads):
            change = jnp.concatenate(
                [correct(h, first).astype(BF16), jnp.zeros((TILE - 16, size), BF16)], axis=0)
            s_send[h] = (s_send[h].astype(F32) + dot(phik[h, :, 0:TILE], change)).astype(BF16)
        for c in range(per):
            send_states(c)

    for c in range(per):
        s_recv[c, r] = s_send[c * group + r]

    lane_head = lax.broadcasted_iota(jnp.int32, (tok, heads * width), 1) // width
    load_qf.wait()
    kt_narrow = kt[...].astype(BF16)
    q_quarter = qf[...] * jnp.asarray(0.25, BF16)
    diagonal = (lax.broadcasted_iota(jnp.int32, (TILE, TILE), 0)
                >= lax.broadcasted_iota(jnp.int32, (TILE, TILE), 1))

    def scores(h):
        lone = jnp.where(lane_head == h, q_quarter, jnp.zeros_like(q_quarter))
        for i in range(tiles):
            t0 = i * TILE
            reach = t0 + TILE
            x = dot(lone[t0:reach, :], kt_narrow[:, 0:reach])
            poly = 1.0 + x * (1.0 + 0.5 * x)
            gap = ccol[t0:reach, h:h + 1] - crow[h:h + 1, 0:reach]
            last = jnp.where(diagonal, gap[:, t0:reach], -1e30)
            if i > 0:
                gap = jnp.concatenate([gap[:, 0:t0], last], axis=1)
            else:
                gap = last
            score = (poly * jnp.exp(gap)).astype(BF16)
            numden[h, t0:reach, :] = dot(score, vw[h, 0:reach, :])

    def fade_of(slab):
        return slab[MIX:MIX + 1, FADE_HI:FADE_HI + 1] + slab[MIX:MIX + 1, FADE_LO:FADE_LO + 1]

    def across(c, slab, last_slab):
        lanes = pl.ds(pl.multiple_of((c * group + r) * size, size), size)
        taps = weight[:, lanes]
        last = last_slab.astype(F32)
        last_1, last_2 = last[LAST_1:LAST_1 + 1, :], last[LAST_2:LAST_2 + 1, :]
        change_0 = taps[1:2, :] * last_1 + taps[2:3, :] * last_2
        change_1 = taps[2:3, :] * last_1
        at_a = jnp.where(slab_row == KEY_0, change_0, jnp.where(slab_row == KEY_1, change_1, 0.0))
        at_0 = jnp.where(slab_row == MIX, change_0, 0.0)
        at_1 = jnp.where(slab_row == MIX, change_1, 0.0)
        out = dot_first(slab, jnp.concatenate([at_a, at_0, at_1], axis=1).astype(BF16))
        rest = out[REST:2 * REST, size:2 * size] + out[2 * REST:3 * REST, 2 * size:3 * size]
        return jnp.concatenate([out[:, 0:size], rest], axis=0)

    def emit(c, earlier):
        def entering(i):
            e = e_group[c, i]
            return (e if earlier is None else e + faded[c * group + i] * earlier).astype(BF16)

        for turn in range(1, group):
            target = turned(turn)
            e_send[c, target] = entering(target)
            e_copy(c, target).start()
        e_recv[c * group + r] = entering(r)

    def gather(c):
        for turn in range(1, group):
            s_arrival(c, turned(turn)).wait_recv()
        running = jnp.zeros((FOLDED, size), F32)
        fades = jnp.ones((1, size), F32)

        def step(j, running, fades):
            block = s_recv[c, j].astype(F32)
            fade = fade_of(block[SLAB:SLAB + 16, :])
            running = fade * running + block
            if j > 0:
                running = running + across(
                    c, s_recv[c, j, SLAB:SLAB + 16, :], s_recv[c, j - 1, SLAB:SLAB + 16, :])
            return running, fades * fade

        for j in range(group - 1):
            e_group[c, j] = running
            faded[c * group + j] = fades
            running, fades = step(j, running, fades)
        e_group[c, group - 1] = running
        faded[c * group + group - 1] = fades

        @pl.when(g < groups - 1)
        def _():
            total, whole = step(group - 1, running, fades)
            whole_hi = whole.astype(BF16).astype(F32)
            slab = total[SLAB:SLAB + 16, :]
            slab = jnp.where((slab_row == MIX) & (slab_lane >= FADE_HI), whole_hi, slab)
            slab = jnp.where((slab_row == MIX) & (slab_lane >= FADE_LO), whole - whole_hi, slab)
            t_send[c] = jnp.concatenate(
                [total[0:SLAB, :], slab, total[SLAB + 16:, :]], axis=0).astype(BF16)
            for target in range(1, groups):
                @pl.when(target > g)
                def _(target=target):
                    t_copy(c, target).start()

    def first_group():
        @pl.when(g == 0)
        def _():
            for c in range(per):
                emit(c, None)

    def pass_on(c):
        @pl.when(g > 0)
        def _():
            t_arrival(c, 0).wait_recv()
            before_group[...] = t_recv[c, 0].astype(F32)
            for source in range(1, groups - 1):
                @pl.when(source < g)
                def _(source=source):
                    t_arrival(c, source).wait_recv()
                    block = t_recv[c, source].astype(F32)
                    before_group[...] = fade_of(block[SLAB:SLAB + 16, :]) * before_group[...] + block
            emit(c, before_group[...])

    row = lax.broadcasted_iota(jnp.int32, (WINDOW, 2 * WINDOW), 0)
    col = lax.broadcasted_iota(jnp.int32, (WINDOW, 2 * WINDOW), 1)
    band = (col > row) & (col <= row + WINDOW)
    steps = tok // WINDOW
    scale = size ** (-0.5)
    ones = jnp.ones((2 * WINDOW, size), BF16)

    def slide(h, start, stop, bias):
        lanes = slice(h * size, (h + 1) * size)
        s = jnp.concatenate([
            dot_t(wq[i * WINDOW:(i + 1) * WINDOW, lanes], kx[i * WINDOW:(i + 2) * WINDOW, lanes])
            for i in range(start, stop)], axis=0)
        s = s * scale + bias
        p = jnp.exp(s - jnp.max(s, axis=1, keepdims=True)).astype(BF16)
        pv = jnp.concatenate([
            dot(p[(i - start) * WINDOW:(i - start + 1) * WINDOW, :],
                jnp.concatenate([vx[i * WINDOW:(i + 2) * WINDOW, lanes], ones], axis=1))
            for i in range(start, stop)], axis=0)
        win[start * WINDOW:stop * WINDOW, lanes] = pv[:, 0:size] * inverse(pv[:, size:2 * size])

    @pl.when((me < n - 1) & (lax.axis_index("head") == 0))
    def _():
        for piece in (1, 2, 3,):
            halo_copy(piece).start()

    load_k.wait()
    load_q.wait()
    bias = jnp.concatenate([jnp.where(band, 0.0, -1e30)] * (steps - 1), axis=0)
    for h in range(0, 2):
        slide(h, 1, steps, bias)

    @pl.when((me < n - 1) & (lax.axis_index("head") == 0))
    def _():
        for piece in (4, 5,):
            halo_copy(piece).start()

    for h in range(2, 4):
        slide(h, 1, steps, bias)

    @pl.when((me < n - 1) & (lax.axis_index("head") == 0))
    def _():
        for piece in (6, 7,):
            halo_copy(piece).start()

    for h in range(4, 6):
        slide(h, 1, steps, bias)

    @pl.when((me < n - 1) & (lax.axis_index("head") == 1))
    def _():
        for piece in (1, 2,):
            halo_copy(piece).start()

    for h in range(6, 8):
        slide(h, 1, steps, bias)

    @pl.when((me < n - 1) & (lax.axis_index("head") == 1))
    def _():
        for piece in (3,):
            halo_copy(piece).start()

    @pl.when((me > 0) & jnp.logical_not(late))
    def _():
        first = first_rows()
        for h in range(heads):
            correct(h, first)

    for h in range(0, 1):
        scores(h)

    @pl.when((me < n - 1) & (lax.axis_index("head") == 1))
    def _():
        for piece in (4, 5,):
            halo_copy(piece).start()

    for h in range(1, 2):
        scores(h)

    @pl.when((me < n - 1) & (lax.axis_index("head") == 1))
    def _():
        for piece in (6, 7,):
            halo_copy(piece).start()

    for h in range(2, 5):
        scores(h)

    gather(0)

    gather(1)

    first_group()

    for h in range(5, 8):
        scores(h)

    pass_on(0)

    pass_on(1)

    qt[...] = qf[...].astype(F32).T
    entering = jnp.exp(crow[...])
    for h in range(heads):
        phiq[h] = fold_features(
            qt[h * width:(h + 1) * width, :], entering[h:h + 1, :], 1.0 / 32, 1.0 / 16, 0.25).T

    @pl.when(me > 0)
    def _():
        for which in range(1, 2 * pieces):
            halo_copy(which).wait_recv()

    first_bias = jnp.where(band & ((col >= WINDOW) | (me > 0)), 0.0, -1e30)
    for h in range(heads):
        slide(h, 0, 1, first_bias)

    picks = jnp.concatenate(
        [jnp.where(slab_row == at, 1.0, 0.0) for at in (NORM, MIX)], axis=1).astype(BF16)
    def finish_head(h):
        lanes = pl.ds(pl.multiple_of(h * size, size), size)
        before = e_recv[h]
        norm = dot_first(before[SLAB:SLAB + 16, :], picks)
        norm = jnp.concatenate([norm[:, 0:size], norm[0:REST, size:2 * size]], axis=0).astype(BF16)
        both = numden[h] + dot(phiq[h], jnp.concatenate([before, norm], axis=1))
        out[:, lanes] = (both[:, 0:size] * inverse(both[:, size:2 * size]) + win[:, lanes]).astype(BF16)

    for c in range(per):
        finish_head(c * group + r)
    for c in range(per):
        for turn in range(1, group):
            e_arrival(c * group + turned(turn)).wait_recv()
        for turn in range(1, group):
            finish_head(c * group + turned(turn))

    @pl.when(me < n - 1)
    def _():
        for which in range(2 * pieces):
            halo_copy(which).wait_send()

    for c in range(per):
        for turn in range(1, group):
            s_copy(c, turned(turn)).wait_send()
            e_copy(c, turned(turn)).wait_send()

        for target in range(1, groups):
            @pl.when(target > g)
            def _(target=target, c=c):
                t_copy(c, target).wait_send()


def solution(mesh):
    n = mesh.shape["seq"]

    def local(q_feat, k_feat, values, win_query, win_key, log_gates, conv_weight):
        tok, channels = values.shape
        heads = log_gates.shape[1]
        size = channels // heads
        width = q_feat.shape[1] // heads
        group = next(s for s in (4, 2, 1) if n % s == 0 and heads % s == 0)
        groups, per = n // group, heads // group
        hbm = pl.BlockSpec(memory_space=pltpu.HBM)
        dma = pltpu.SemaphoreType.DMA
        block = (FOLDED, size)
        operands = (q_feat, k_feat, log_gates.T, conv_weight, values, win_key, win_query)
        return pl.pallas_call(
            functools.partial(kernel, n, group, heads, size, width),
            out_shape=jax.ShapeDtypeStruct((tok, channels), BF16),
            in_specs=[hbm] * 7,
            out_specs=pl.BlockSpec(memory_space=pltpu.VMEM),
            scratch_shapes=[
                pltpu.VMEM(q_feat.shape, BF16),
                pltpu.VMEM(k_feat.shape, BF16),
                pltpu.VMEM((heads, tok), F32),
                pltpu.VMEM(conv_weight.shape, F32),
                pltpu.VMEM((tok + WINDOW, channels), BF16),
                pltpu.VMEM((tok + WINDOW, channels), BF16),
                pltpu.VMEM((tok, channels), BF16),
                pltpu.VMEM((tok + 8, channels), F32),
                pltpu.VMEM((heads, tok, 2 * size), BF16),
                pltpu.VMEM((heads * width, tok), F32),
                pltpu.VMEM((heads * width, tok), F32),
                pltpu.VMEM((heads, FOLDED, tok), BF16),
                pltpu.VMEM((heads, tok, FOLDED), BF16),
                pltpu.VMEM((heads, tok, 2 * size), F32),
                pltpu.VMEM((tok, channels), F32),
                pltpu.VMEM((tok, 128), F32),
                pltpu.VMEM((heads, tok), F32),
                pltpu.VMEM((heads,) + block, BF16),
                pltpu.VMEM((per, group) + block, BF16),
                pltpu.VMEM((per, group) + block, F32),
                pltpu.VMEM((heads, 1, size), F32),
                pltpu.VMEM(block, F32),
                pltpu.VMEM((per,) + block, BF16),
                pltpu.VMEM((per, groups) + block, BF16),
                pltpu.VMEM((per, group) + block, BF16),
                pltpu.VMEM((heads,) + block, BF16),
                dma((7,)), dma((2 * WINDOW // PIECE,)), dma((2 * WINDOW // PIECE,)),
                dma((heads,)), dma((per, group)), dma((per, groups)), dma((per, groups)),
                dma((per, group)), dma((heads,)),
            ],
            compiler_params=pltpu.CompilerParams(
                collective_id=0, has_side_effects=True, vmem_limit_bytes=40 * 1024 * 1024),
        )(*[pltpu.with_memory_space_constraint(x, pltpu.HBM) for x in operands])

    shard = P(("grp", "seq"), "head")
    return jax.shard_map(
        local, mesh=mesh, in_specs=(shard,) * 6 + (P(None, "head"),), out_specs=shard, check_vma=False)
```

```python
import functools

import jax
import jax.numpy as jnp
from jax import lax
from jax.experimental import pallas as pl
from jax.experimental.pallas import tpu as pltpu
from jax.sharding import PartitionSpec as P

WINDOW = 64
TILE = 128
FOLDED = 160
SLAB = 128
NORM, KEY_0, KEY_1, MIX, LAST_2, LAST_1 = 9, 10, 11, 12, 13, 14
REST = FOLDED - SLAB
FADE_HI, FADE_LO = 96, 112
EARLY = 4
PIECE = 16
F32 = jnp.float32
BF16 = jnp.bfloat16
MESH = pl.DeviceIdType.MESH


def dot(a, b):
    return lax.dot_general(a, b, (((1,), (0,)), ((), ())), preferred_element_type=F32)


def dot_t(a, b):
    return lax.dot_general(a, b, (((1,), (1,)), ((), ())), preferred_element_type=F32)


def dot_first(a, b):
    return lax.dot_general(a, b, (((0,), (0,)), ((), ())), preferred_element_type=F32)


def inverse(x):
    guess = pl.reciprocal(x, approx=True)
    return guess * (2.0 - x * guess)


def fold_features(x, level, square_scale, pair_scale, linear_scale):
    rows = lax.broadcasted_iota(jnp.int32, x.shape, 0)
    levelled = x * level
    scaled = levelled * pair_scale
    parts = [(levelled * square_scale) * x]
    for step in range(1, 8):
        parts.append(scaled * pltpu.roll(x, 16 - step, 0))
    half = scaled * pltpu.roll(x, 8, 0)
    parts.append(jnp.where(rows < 8, half, jnp.where(rows == 8, level, 0.0)))
    parts.append(levelled * linear_scale)
    return jnp.concatenate([part.astype(BF16) for part in parts], axis=0)


def kernel(
    n, group, heads, size, width,
    q_feat, k_feat, log_gates, conv_weight, values, win_key, win_query,
    out,
    qf, kf, gates, weight,
    vx, kx, wq, vf, vw, qt, kt, phik, phiq, numden, win, ccol, crow,
    s_send, s_recv, e_group, faded, before_group, t_send, t_recv, e_send, e_recv,
    in_sem, halo_send, halo_recv, ss_sem, sr_sem, ts_sem, tr_sem, es_sem, er_sem,
):
    me = lax.axis_index("seq")
    groups = n // group
    per = heads // group
    g = me // group
    r = lax.rem(me, group)
    tok = qf.shape[0]
    tiles = tok // TILE
    tail = WINDOW
    pieces = tail // PIECE

    loads = [
        pltpu.make_async_copy(log_gates, gates, in_sem.at[0]),
        pltpu.make_async_copy(k_feat, kf, in_sem.at[1]),
        pltpu.make_async_copy(values, vx.at[pl.ds(tail, tok)], in_sem.at[2]),
        pltpu.make_async_copy(conv_weight, weight, in_sem.at[3]),
        pltpu.make_async_copy(q_feat, qf, in_sem.at[4]),
        pltpu.make_async_copy(win_key, kx.at[pl.ds(tail, tok)], in_sem.at[5]),
        pltpu.make_async_copy(win_query, wq, in_sem.at[6]),
    ]
    for load in loads[:5]:
        load.start()
    load_g, load_kf, load_v, load_w, load_qf, load_k, load_q = loads

    barrier = pltpu.get_barrier_semaphore()

    def greet(peer):
        pl.semaphore_signal(barrier, inc=1, device_id={"seq": peer}, device_id_type=MESH)

    for turn in range(1, group):
        greet(g * group + lax.rem(r + turn, group))
    for turn in range(1, groups):
        greet(lax.rem(me + turn * group, n))
    across_next = (r == group - 1) & (g < groups - 1)
    across_prev = (r == 0) & (g > 0)

    @pl.when(across_next)
    def _():
        greet(me + 1)

    @pl.when(across_prev)
    def _():
        greet(me - 1)

    @pl.when(me == 0)
    def _():
        vx[0:tail, :] = jnp.zeros((tail, heads * size), BF16)
        kx[0:tail, :] = jnp.zeros((tail, heads * size), BF16)

    vf[0:8, :] = jnp.zeros((8, heads * size), F32)
    nxt = lax.rem(me + 1, n)

    def halo_copy(which):
        source, target = ((values, vx), (win_key, kx))[which // pieces]
        start = tail - PIECE * (which % pieces + 1)
        return pltpu.make_async_remote_copy(
            source.at[pl.ds(tok - tail + start, PIECE)], target.at[pl.ds(start, PIECE)],
            halo_send.at[which], halo_recv.at[which], device_id={"seq": nxt}, device_id_type=MESH)

    def send_halo(*which):
        @pl.when(me < n - 1)
        def _():
            for piece in which:
                halo_copy(piece).start()

    def turned(turn):
        return lax.rem(r + turn, group)

    def s_copy(c, owner):
        return pltpu.make_async_remote_copy(
            s_send.at[c * group + owner], s_recv.at[c, r], ss_sem.at[c * group + owner], sr_sem.at[c, r],
            device_id={"seq": g * group + owner}, device_id_type=MESH)

    def s_arrival(c, source):
        return pltpu.make_async_remote_copy(
            s_send.at[c * group], s_recv.at[c, source], ss_sem.at[c * group], sr_sem.at[c, source],
            device_id={"seq": g * group + source}, device_id_type=MESH)

    def t_copy(c, target):
        return pltpu.make_async_remote_copy(
            t_send.at[c], t_recv.at[c, g], ts_sem.at[c, target], tr_sem.at[c, g],
            device_id={"seq": target * group + r}, device_id_type=MESH)

    def t_arrival(c, source):
        return pltpu.make_async_remote_copy(
            t_send.at[c], t_recv.at[c, source], ts_sem.at[c, source], tr_sem.at[c, source],
            device_id={"seq": source * group + r}, device_id_type=MESH)

    def e_copy(c, target):
        return pltpu.make_async_remote_copy(
            e_send.at[c, target], e_recv.at[c * group + r], es_sem.at[c, target], er_sem.at[c * group + r],
            device_id={"seq": g * group + target}, device_id_type=MESH)

    def e_arrival(h):
        return pltpu.make_async_remote_copy(
            e_send.at[0, 0], e_recv.at[h], es_sem.at[0, 0], er_sem.at[h],
            device_id={"seq": g * group + lax.rem(h, group)}, device_id_type=MESH)

    before_or_at = jnp.where(
        lax.broadcasted_iota(jnp.int32, (tok, tok), 0) <= lax.broadcasted_iota(jnp.int32, (tok, tok), 1),
        1.0, 0.0).astype(BF16)
    load_g.wait()
    upper = gates[...].astype(BF16)
    rest = gates[...] - upper.astype(F32)
    middle = rest.astype(BF16)
    lowest = (rest - middle.astype(F32)).astype(BF16)
    total = dot(jnp.concatenate([upper, middle, lowest], axis=0), before_or_at)
    total = total[0:heads] + (total[heads:2 * heads] + total[2 * heads:3 * heads])
    crow[...] = total
    ccol[...] = jnp.concatenate([total, jnp.zeros((128 - heads, tok), F32)], axis=0).T
    keep_row = jnp.exp(total[:, tok - 1:tok] - total)
    finish = jnp.exp(total[:, tok - 1:tok])
    finish_hi = finish.astype(BF16).astype(F32)
    finish_lo = finish - finish_hi

    load_kf.wait()
    kt[...] = kf[...].astype(F32).T
    for h in range(heads):
        phik[h] = fold_features(
            kt[h * width:(h + 1) * width, :], keep_row[h:h + 1, :], 1.0, 1.0, 1.0)

    load_w.wait()
    load_v.wait()
    loads[5].start()
    loads[6].start()
    slab_row = lax.broadcasted_iota(jnp.int32, (16, size), 0)
    slab_lane = lax.broadcasted_iota(jnp.int32, (16, size), 1)
    probe_row = lax.broadcasted_iota(jnp.int32, (16, tok), 0)
    probe_lane = lax.broadcasted_iota(jnp.int32, (16, tok), 1)
    probes = jnp.where((probe_row == 0) | (probe_lane == probe_row - 1), 1.0, 0.0).astype(BF16)
    late = (r == 0) & (g > 0)

    def state(h):
        lanes = slice(h * size, (h + 1) * size)
        current = vx[tail:tail + tok, lanes].astype(F32)
        vf[8:8 + tok, lanes] = current
        conv = weight[0:1, lanes] * current
        for tap in range(1, weight.shape[0]):
            conv = conv + weight[tap:tap + 1, lanes] * vf[8 - tap:8 - tap + tok, lanes]
        conv = conv.astype(BF16)
        vw[h, :, 0:size] = conv
        vw[h, :, size:2 * size] = jnp.ones((tok, size), BF16)
        folded = dot(phik[h], conv)
        probed = dot_t(probes, phik[h])
        ends = jnp.concatenate([probed[:, SLAB:FOLDED], jnp.zeros((16, SLAB - REST), F32)], axis=1)
        mix = (ends[0:1, :] + pltpu.roll(ends, REST, 1)[1:2, :] + pltpu.roll(ends, 2 * REST, 1)[2:3, :])
        mix = jnp.where(slab_lane[0:1, :] >= FADE_HI, finish_hi[h:h + 1, :], mix)
        mix = jnp.where(slab_lane[0:1, :] >= FADE_LO, finish_lo[h:h + 1, :], mix)
        slab = folded[SLAB:SLAB + 16, :]
        for at, line in ((NORM, probed[0:1, 0:SLAB]), (KEY_0, probed[1:2, 0:SLAB]), (KEY_1, probed[2:3, 0:SLAB]),
                         (MIX, mix), (LAST_2, current[tok - 2:tok - 1, :]), (LAST_1, current[tok - 1:tok, :])):
            slab = jnp.where(slab_row == at, line, slab)
        s_send[h] = jnp.concatenate([folded[0:SLAB, :], slab, folded[SLAB + 16:, :]], axis=0).astype(BF16)

    def send_states(c):
        for turn in range(1, group):
            s_copy(c, turned(turn)).start()

    def correct(h, first):
        lanes = slice(h * size, (h + 1) * size)
        change = first[:, lanes].astype(F32) - vw[h, 0:16, 0:size].astype(F32)
        vw[h, 0:16, 0:size] = first[:, lanes]
        return change

    def first_rows():
        halo_copy(0).wait_recv()
        vf[0:8, :] = vx[tail - 16:tail, :].astype(F32)[8:16, :]
        first = weight[0:1, :] * vf[8:24, :]
        for tap in range(1, weight.shape[0]):
            first = first + weight[tap:tap + 1, :] * vf[8 - tap:24 - tap, :]
        return first.astype(BF16)

    for h in range(EARLY):
        state(h)
    pl.semaphore_wait(
        barrier, (group - 1) + (groups - 1) + across_next.astype(jnp.int32) + across_prev.astype(jnp.int32))

    send_halo(0)

    for c in range(per):
        for h in range(c * group, (c + 1) * group):
            if h >= EARLY:
                state(h)

        @pl.when(jnp.logical_not(late))
        def _(c=c):
            send_states(c)

    lane_head = lax.broadcasted_iota(jnp.int32, (tok, heads * width), 1) // width
    load_qf.wait()
    kt_narrow = kt[...].astype(BF16)
    q_quarter = qf[...] * jnp.asarray(0.25, BF16)
    diagonal = (lax.broadcasted_iota(jnp.int32, (TILE, TILE), 0)
                >= lax.broadcasted_iota(jnp.int32, (TILE, TILE), 1))

    def scores(h):
        lone = jnp.where(lane_head == h, q_quarter, jnp.zeros_like(q_quarter))
        for i in range(tiles):
            t0 = i * TILE
            reach = t0 + TILE
            x = dot(lone[t0:reach, :], kt_narrow[:, 0:reach])
            poly = 1.0 + x * (1.0 + 0.5 * x)
            gap = ccol[t0:reach, h:h + 1] - crow[h:h + 1, 0:reach]
            last = jnp.where(diagonal, gap[:, t0:reach], -1e30)
            if i > 0:
                gap = jnp.concatenate([gap[:, 0:t0], last], axis=1)
            else:
                gap = last
            score = (poly * jnp.exp(gap)).astype(BF16)
            numden[h, t0:reach, :] = dot(score, vw[h, 0:reach, :])

    def fade_of(slab):
        return slab[MIX:MIX + 1, FADE_HI:FADE_HI + 1] + slab[MIX:MIX + 1, FADE_LO:FADE_LO + 1]

    def across(c, slab, last_slab):
        lanes = pl.ds(pl.multiple_of((c * group + r) * size, size), size)
        taps = weight[:, lanes]
        last = last_slab.astype(F32)
        last_1, last_2 = last[LAST_1:LAST_1 + 1, :], last[LAST_2:LAST_2 + 1, :]
        change_0 = taps[1:2, :] * last_1 + taps[2:3, :] * last_2
        change_1 = taps[2:3, :] * last_1
        at_a = jnp.where(slab_row == KEY_0, change_0, jnp.where(slab_row == KEY_1, change_1, 0.0))
        at_0 = jnp.where(slab_row == MIX, change_0, 0.0)
        at_1 = jnp.where(slab_row == MIX, change_1, 0.0)
        out = dot_first(slab, jnp.concatenate([at_a, at_0, at_1], axis=1).astype(BF16))
        rest = out[REST:2 * REST, size:2 * size] + out[2 * REST:3 * REST, 2 * size:3 * size]
        return jnp.concatenate([out[:, 0:size], rest], axis=0)

    def emit(c, earlier):
        def entering(i):
            e = e_group[c, i]
            return (e if earlier is None else e + faded[c * group + i] * earlier).astype(BF16)

        for turn in range(1, group):
            target = turned(turn)
            e_send[c, target] = entering(target)
            e_copy(c, target).start()
        e_recv[c * group + r] = entering(r)

    def gather(c):
        for turn in range(1, group):
            s_arrival(c, turned(turn)).wait_recv()
        running = jnp.zeros((FOLDED, size), F32)
        fades = jnp.ones((1, size), F32)

        def step(j, running, fades):
            block = s_recv[c, j].astype(F32)
            fade = fade_of(block[SLAB:SLAB + 16, :])
            running = fade * running + block
            if j > 0:
                running = running + across(
                    c, s_recv[c, j, SLAB:SLAB + 16, :], s_recv[c, j - 1, SLAB:SLAB + 16, :])
            return running, fades * fade

        for j in range(group - 1):
            e_group[c, j] = running
            faded[c * group + j] = fades
            running, fades = step(j, running, fades)
        e_group[c, group - 1] = running
        faded[c * group + group - 1] = fades

        @pl.when(g < groups - 1)
        def _():
            total, whole = step(group - 1, running, fades)
            whole_hi = whole.astype(BF16).astype(F32)
            slab = total[SLAB:SLAB + 16, :]
            slab = jnp.where((slab_row == MIX) & (slab_lane >= FADE_HI), whole_hi, slab)
            slab = jnp.where((slab_row == MIX) & (slab_lane >= FADE_LO), whole - whole_hi, slab)
            t_send[c] = jnp.concatenate(
                [total[0:SLAB, :], slab, total[SLAB + 16:, :]], axis=0).astype(BF16)
            for target in range(1, groups):
                @pl.when(target > g)
                def _(target=target):
                    t_copy(c, target).start()

    def first_group():
        @pl.when(g == 0)
        def _():
            for c in range(per):
                emit(c, None)

    def pass_on(c):
        @pl.when(g > 0)
        def _():
            t_arrival(c, 0).wait_recv()
            before_group[...] = t_recv[c, 0].astype(F32)
            for source in range(1, groups - 1):
                @pl.when(source < g)
                def _(source=source):
                    t_arrival(c, source).wait_recv()
                    block = t_recv[c, source].astype(F32)
                    before_group[...] = fade_of(block[SLAB:SLAB + 16, :]) * before_group[...] + block
            emit(c, before_group[...])

    row = lax.broadcasted_iota(jnp.int32, (WINDOW, 2 * WINDOW), 0)
    col = lax.broadcasted_iota(jnp.int32, (WINDOW, 2 * WINDOW), 1)
    band = (col > row) & (col <= row + WINDOW)
    steps = tok // WINDOW
    scale = size ** (-0.5)
    ones = jnp.ones((2 * WINDOW, size), BF16)

    def slide(h, start, stop, bias):
        lanes = slice(h * size, (h + 1) * size)
        s = jnp.concatenate([
            dot_t(wq[i * WINDOW:(i + 1) * WINDOW, lanes], kx[i * WINDOW:(i + 2) * WINDOW, lanes])
            for i in range(start, stop)], axis=0)
        s = s * scale + bias
        p = jnp.exp(s - jnp.max(s, axis=1, keepdims=True)).astype(BF16)
        pv = jnp.concatenate([
            dot(p[(i - start) * WINDOW:(i - start + 1) * WINDOW, :],
                jnp.concatenate([vx[i * WINDOW:(i + 2) * WINDOW, lanes], ones], axis=1))
            for i in range(start, stop)], axis=0)
        win[start * WINDOW:stop * WINDOW, lanes] = pv[:, 0:size] * inverse(pv[:, size:2 * size])

    @pl.when((me < n - 1) & (lax.axis_index("head") == 0))
    def _():
        for piece in (1, 2, 3,):
            halo_copy(piece).start()

    load_k.wait()
    load_q.wait()
    bias = jnp.concatenate([jnp.where(band, 0.0, -1e30)] * (steps - 1), axis=0)
    for h in range(0, 1):
        slide(h, 1, steps, bias)

    @pl.when(late)
    def _():
        first = first_rows()
        for h in range(heads):
            change = jnp.concatenate(
                [correct(h, first).astype(BF16), jnp.zeros((TILE - 16, size), BF16)], axis=0)
            s_send[h] = (s_send[h].astype(F32) + dot(phik[h, :, 0:TILE], change)).astype(BF16)
        for c in range(per):
            send_states(c)

    for c in range(per):
        s_recv[c, r] = s_send[c * group + r]

    @pl.when((me < n - 1) & (lax.axis_index("head") == 0))
    def _():
        for piece in (4, 5,):
            halo_copy(piece).start()

    for h in range(1, 2):
        slide(h, 1, steps, bias)

    @pl.when((me < n - 1) & (lax.axis_index("head") == 0))
    def _():
        for piece in (6, 7,):
            halo_copy(piece).start()

    for h in range(2, 4):
        slide(h, 1, steps, bias)

    @pl.when((me < n - 1) & (lax.axis_index("head") == 1))
    def _():
        for piece in (1, 2,):
            halo_copy(piece).start()

    for h in range(4, 6):
        slide(h, 1, steps, bias)

    @pl.when((me < n - 1) & (lax.axis_index("head") == 1))
    def _():
        for piece in (3, 4,):
            halo_copy(piece).start()

    for h in range(6, 8):
        slide(h, 1, steps, bias)

    @pl.when((me > 0) & jnp.logical_not(late))
    def _():
        first = first_rows()
        for h in range(heads):
            correct(h, first)

    @pl.when((me < n - 1) & (lax.axis_index("head") == 1))
    def _():
        for piece in (5,):
            halo_copy(piece).start()

    for h in range(0, 1):
        scores(h)

    @pl.when((me < n - 1) & (lax.axis_index("head") == 1))
    def _():
        for piece in (6, 7,):
            halo_copy(piece).start()

    for h in range(1, 5):
        scores(h)

    gather(0)

    gather(1)

    first_group()

    for h in range(5, 7):
        scores(h)

    pass_on(0)

    for h in range(7, 8):
        scores(h)

    pass_on(1)

    qt[...] = qf[...].astype(F32).T
    entering = jnp.exp(crow[...])
    for h in range(heads):
        phiq[h] = fold_features(
            qt[h * width:(h + 1) * width, :], entering[h:h + 1, :], 1.0 / 32, 1.0 / 16, 0.25).T

    @pl.when(me > 0)
    def _():
        for which in range(1, 2 * pieces):
            halo_copy(which).wait_recv()

    first_bias = jnp.where(band & ((col >= WINDOW) | (me > 0)), 0.0, -1e30)
    for h in range(heads):
        slide(h, 0, 1, first_bias)

    picks = jnp.concatenate(
        [jnp.where(slab_row == at, 1.0, 0.0) for at in (NORM, MIX)], axis=1).astype(BF16)
    def finish_head(h):
        lanes = pl.ds(pl.multiple_of(h * size, size), size)
        before = e_recv[h]
        norm = dot_first(before[SLAB:SLAB + 16, :], picks)
        norm = jnp.concatenate([norm[:, 0:size], norm[0:REST, size:2 * size]], axis=0).astype(BF16)
        both = numden[h] + dot(phiq[h], jnp.concatenate([before, norm], axis=1))
        out[:, lanes] = (both[:, 0:size] * inverse(both[:, size:2 * size]) + win[:, lanes]).astype(BF16)

    for c in range(per):
        finish_head(c * group + r)
    for c in range(per):
        for turn in range(1, group):
            e_arrival(c * group + turned(turn)).wait_recv()
        for turn in range(1, group):
            finish_head(c * group + turned(turn))

    @pl.when(me < n - 1)
    def _():
        for which in range(2 * pieces):
            halo_copy(which).wait_send()

    for c in range(per):
        for turn in range(1, group):
            s_copy(c, turned(turn)).wait_send()
            e_copy(c, turned(turn)).wait_send()

        for target in range(1, groups):
            @pl.when(target > g)
            def _(target=target, c=c):
                t_copy(c, target).wait_send()


def solution(mesh):
    n = mesh.shape["seq"]

    def local(q_feat, k_feat, values, win_query, win_key, log_gates, conv_weight):
        tok, channels = values.shape
        heads = log_gates.shape[1]
        size = channels // heads
        width = q_feat.shape[1] // heads
        group = next(s for s in (4, 2, 1) if n % s == 0 and heads % s == 0)
        groups, per = n // group, heads // group
        hbm = pl.BlockSpec(memory_space=pltpu.HBM)
        dma = pltpu.SemaphoreType.DMA
        block = (FOLDED, size)
        operands = (q_feat, k_feat, log_gates.T, conv_weight, values, win_key, win_query)
        return pl.pallas_call(
            functools.partial(kernel, n, group, heads, size, width),
            out_shape=jax.ShapeDtypeStruct((tok, channels), BF16),
            in_specs=[hbm] * 7,
            out_specs=pl.BlockSpec(memory_space=pltpu.VMEM),
            scratch_shapes=[
                pltpu.VMEM(q_feat.shape, BF16),
                pltpu.VMEM(k_feat.shape, BF16),
                pltpu.VMEM((heads, tok), F32),
                pltpu.VMEM(conv_weight.shape, F32),
                pltpu.VMEM((tok + WINDOW, channels), BF16),
                pltpu.VMEM((tok + WINDOW, channels), BF16),
                pltpu.VMEM((tok, channels), BF16),
                pltpu.VMEM((tok + 8, channels), F32),
                pltpu.VMEM((heads, tok, 2 * size), BF16),
                pltpu.VMEM((heads * width, tok), F32),
                pltpu.VMEM((heads * width, tok), F32),
                pltpu.VMEM((heads, FOLDED, tok), BF16),
                pltpu.VMEM((heads, tok, FOLDED), BF16),
                pltpu.VMEM((heads, tok, 2 * size), F32),
                pltpu.VMEM((tok, channels), F32),
                pltpu.VMEM((tok, 128), F32),
                pltpu.VMEM((heads, tok), F32),
                pltpu.VMEM((heads,) + block, BF16),
                pltpu.VMEM((per, group) + block, BF16),
                pltpu.VMEM((per, group) + block, F32),
                pltpu.VMEM((heads, 1, size), F32),
                pltpu.VMEM(block, F32),
                pltpu.VMEM((per,) + block, BF16),
                pltpu.VMEM((per, groups) + block, BF16),
                pltpu.VMEM((per, group) + block, BF16),
                pltpu.VMEM((heads,) + block, BF16),
                dma((7,)), dma((2 * WINDOW // PIECE,)), dma((2 * WINDOW // PIECE,)),
                dma((heads,)), dma((per, group)), dma((per, groups)), dma((per, groups)),
                dma((per, group)), dma((heads,)),
            ],
            compiler_params=pltpu.CompilerParams(
                collective_id=0, has_side_effects=True, vmem_limit_bytes=40 * 1024 * 1024),
        )(*[pltpu.with_memory_space_constraint(x, pltpu.HBM) for x in operands])

    shard = P(("grp", "seq"), "head")
    return jax.shard_map(
        local, mesh=mesh, in_specs=(shard,) * 6 + (P(None, "head"),), out_specs=shard, check_vma=False)
```

```python
import functools

import jax
import jax.numpy as jnp
from jax import lax
from jax.experimental import pallas as pl
from jax.experimental.pallas import tpu as pltpu
from jax.sharding import PartitionSpec as P

WINDOW = 64
TILE = 128
FOLDED = 160
SLAB = 128
NORM, KEY_0, KEY_1, MIX, LAST_2, LAST_1 = 9, 10, 11, 12, 13, 14
REST = FOLDED - SLAB
FADE_HI, FADE_LO = 96, 112
EARLY = 4
PIECE = 16
F32 = jnp.float32
BF16 = jnp.bfloat16
MESH = pl.DeviceIdType.MESH


def dot(a, b):
    return lax.dot_general(a, b, (((1,), (0,)), ((), ())), preferred_element_type=F32)


def dot_t(a, b):
    return lax.dot_general(a, b, (((1,), (1,)), ((), ())), preferred_element_type=F32)


def dot_first(a, b):
    return lax.dot_general(a, b, (((0,), (0,)), ((), ())), preferred_element_type=F32)


def inverse(x):
    guess = pl.reciprocal(x, approx=True)
    return guess * (2.0 - x * guess)


def fold_features(x, level, square_scale, pair_scale, linear_scale):
    rows = lax.broadcasted_iota(jnp.int32, x.shape, 0)
    levelled = x * level
    scaled = levelled * pair_scale
    parts = [(levelled * square_scale) * x]
    for step in range(1, 8):
        parts.append(scaled * pltpu.roll(x, 16 - step, 0))
    half = scaled * pltpu.roll(x, 8, 0)
    parts.append(jnp.where(rows < 8, half, jnp.where(rows == 8, level, 0.0)))
    parts.append(levelled * linear_scale)
    return jnp.concatenate([part.astype(BF16) for part in parts], axis=0)


def kernel(
    n, group, heads, size, width,
    q_feat, k_feat, log_gates, conv_weight, values, win_key, win_query,
    out,
    qf, kf, gates, weight,
    vx, kx, wq, vf, vw, qt, kt, phik, phiq, numden, win, ccol, crow,
    s_send, s_recv, e_group, faded, before_group, t_send, t_recv, e_send, e_recv,
    in_sem, halo_send, halo_recv, ss_sem, sr_sem, ts_sem, tr_sem, es_sem, er_sem,
):
    me = lax.axis_index("seq")
    groups = n // group
    per = heads // group
    g = me // group
    r = lax.rem(me, group)
    tok = qf.shape[0]
    tiles = tok // TILE
    tail = WINDOW
    pieces = tail // PIECE

    loads = [
        pltpu.make_async_copy(log_gates, gates, in_sem.at[0]),
        pltpu.make_async_copy(k_feat, kf, in_sem.at[1]),
        pltpu.make_async_copy(values, vx.at[pl.ds(tail, tok)], in_sem.at[2]),
        pltpu.make_async_copy(conv_weight, weight, in_sem.at[3]),
        pltpu.make_async_copy(q_feat, qf, in_sem.at[4]),
        pltpu.make_async_copy(win_key, kx.at[pl.ds(tail, tok)], in_sem.at[5]),
        pltpu.make_async_copy(win_query, wq, in_sem.at[6]),
    ]
    for load in loads[:5]:
        load.start()
    load_g, load_kf, load_v, load_w, load_qf, load_k, load_q = loads

    barrier = pltpu.get_barrier_semaphore()

    def greet(peer):
        pl.semaphore_signal(barrier, inc=1, device_id={"seq": peer}, device_id_type=MESH)

    for turn in range(1, group):
        greet(g * group + lax.rem(r + turn, group))
    for turn in range(1, groups):
        greet(lax.rem(me + turn * group, n))
    across_next = (r == group - 1) & (g < groups - 1)
    across_prev = (r == 0) & (g > 0)

    @pl.when(across_next)
    def _():
        greet(me + 1)

    @pl.when(across_prev)
    def _():
        greet(me - 1)

    @pl.when(me == 0)
    def _():
        vx[0:tail, :] = jnp.zeros((tail, heads * size), BF16)
        kx[0:tail, :] = jnp.zeros((tail, heads * size), BF16)

    vf[0:8, :] = jnp.zeros((8, heads * size), F32)
    nxt = lax.rem(me + 1, n)

    def halo_copy(which):
        source, target = ((values, vx), (win_key, kx))[which // pieces]
        start = tail - PIECE * (which % pieces + 1)
        return pltpu.make_async_remote_copy(
            source.at[pl.ds(tok - tail + start, PIECE)], target.at[pl.ds(start, PIECE)],
            halo_send.at[which], halo_recv.at[which], device_id={"seq": nxt}, device_id_type=MESH)

    def send_halo(*which):
        @pl.when(me < n - 1)
        def _():
            for piece in which:
                halo_copy(piece).start()

    def turned(turn):
        return lax.rem(r + turn, group)

    def s_copy(c, owner):
        return pltpu.make_async_remote_copy(
            s_send.at[c * group + owner], s_recv.at[c, r], ss_sem.at[c * group + owner], sr_sem.at[c, r],
            device_id={"seq": g * group + owner}, device_id_type=MESH)

    def s_arrival(c, source):
        return pltpu.make_async_remote_copy(
            s_send.at[c * group], s_recv.at[c, source], ss_sem.at[c * group], sr_sem.at[c, source],
            device_id={"seq": g * group + source}, device_id_type=MESH)

    def t_copy(c, target):
        return pltpu.make_async_remote_copy(
            t_send.at[c], t_recv.at[c, g], ts_sem.at[c, target], tr_sem.at[c, g],
            device_id={"seq": target * group + r}, device_id_type=MESH)

    def t_arrival(c, source):
        return pltpu.make_async_remote_copy(
            t_send.at[c], t_recv.at[c, source], ts_sem.at[c, source], tr_sem.at[c, source],
            device_id={"seq": source * group + r}, device_id_type=MESH)

    def e_copy(c, target):
        return pltpu.make_async_remote_copy(
            e_send.at[c, target], e_recv.at[c * group + r], es_sem.at[c, target], er_sem.at[c * group + r],
            device_id={"seq": g * group + target}, device_id_type=MESH)

    def e_arrival(h):
        return pltpu.make_async_remote_copy(
            e_send.at[0, 0], e_recv.at[h], es_sem.at[0, 0], er_sem.at[h],
            device_id={"seq": g * group + lax.rem(h, group)}, device_id_type=MESH)

    before_or_at = jnp.where(
        lax.broadcasted_iota(jnp.int32, (tok, tok), 0) <= lax.broadcasted_iota(jnp.int32, (tok, tok), 1),
        1.0, 0.0).astype(BF16)
    load_g.wait()
    upper = gates[...].astype(BF16)
    rest = gates[...] - upper.astype(F32)
    middle = rest.astype(BF16)
    lowest = (rest - middle.astype(F32)).astype(BF16)
    total = dot(jnp.concatenate([upper, middle, lowest], axis=0), before_or_at)
    total = total[0:heads] + (total[heads:2 * heads] + total[2 * heads:3 * heads])
    crow[...] = total
    ccol[...] = jnp.concatenate([total, jnp.zeros((128 - heads, tok), F32)], axis=0).T
    keep_row = jnp.exp(total[:, tok - 1:tok] - total)
    finish = jnp.exp(total[:, tok - 1:tok])
    finish_hi = finish.astype(BF16).astype(F32)
    finish_lo = finish - finish_hi

    load_kf.wait()
    kt[...] = kf[...].astype(F32).T
    for h in range(heads):
        phik[h] = fold_features(
            kt[h * width:(h + 1) * width, :], keep_row[h:h + 1, :], 1.0, 1.0, 1.0)

    load_w.wait()
    load_v.wait()
    loads[5].start()
    loads[6].start()
    slab_row = lax.broadcasted_iota(jnp.int32, (16, size), 0)
    slab_lane = lax.broadcasted_iota(jnp.int32, (16, size), 1)
    probe_row = lax.broadcasted_iota(jnp.int32, (16, tok), 0)
    probe_lane = lax.broadcasted_iota(jnp.int32, (16, tok), 1)
    probes = jnp.where((probe_row == 0) | (probe_lane == probe_row - 1), 1.0, 0.0).astype(BF16)
    late = (r == 0) & (g > 0)

    def state(h):
        lanes = slice(h * size, (h + 1) * size)
        current = vx[tail:tail + tok, lanes].astype(F32)
        vf[8:8 + tok, lanes] = current
        conv = weight[0:1, lanes] * current
        for tap in range(1, weight.shape[0]):
            conv = conv + weight[tap:tap + 1, lanes] * vf[8 - tap:8 - tap + tok, lanes]
        conv = conv.astype(BF16)
        vw[h, :, 0:size] = conv
        vw[h, :, size:2 * size] = jnp.ones((tok, size), BF16)
        folded = dot(phik[h], conv)
        probed = dot_t(probes, phik[h])
        ends = jnp.concatenate([probed[:, SLAB:FOLDED], jnp.zeros((16, SLAB - REST), F32)], axis=1)
        mix = (ends[0:1, :] + pltpu.roll(ends, REST, 1)[1:2, :] + pltpu.roll(ends, 2 * REST, 1)[2:3, :])
        mix = jnp.where(slab_lane[0:1, :] >= FADE_HI, finish_hi[h:h + 1, :], mix)
        mix = jnp.where(slab_lane[0:1, :] >= FADE_LO, finish_lo[h:h + 1, :], mix)
        slab = folded[SLAB:SLAB + 16, :]
        for at, line in ((NORM, probed[0:1, 0:SLAB]), (KEY_0, probed[1:2, 0:SLAB]), (KEY_1, probed[2:3, 0:SLAB]),
                         (MIX, mix), (LAST_2, current[tok - 2:tok - 1, :]), (LAST_1, current[tok - 1:tok, :])):
            slab = jnp.where(slab_row == at, line, slab)
        s_send[h] = jnp.concatenate([folded[0:SLAB, :], slab, folded[SLAB + 16:, :]], axis=0).astype(BF16)

    def send_states(c):
        for turn in range(1, group):
            s_copy(c, turned(turn)).start()

    def correct(h, first):
        lanes = slice(h * size, (h + 1) * size)
        change = first[:, lanes].astype(F32) - vw[h, 0:16, 0:size].astype(F32)
        vw[h, 0:16, 0:size] = first[:, lanes]
        return change

    def first_rows():
        halo_copy(0).wait_recv()
        vf[0:8, :] = vx[tail - 16:tail, :].astype(F32)[8:16, :]
        first = weight[0:1, :] * vf[8:24, :]
        for tap in range(1, weight.shape[0]):
            first = first + weight[tap:tap + 1, :] * vf[8 - tap:24 - tap, :]
        return first.astype(BF16)

    for h in range(EARLY):
        state(h)
    pl.semaphore_wait(
        barrier, (group - 1) + (groups - 1) + across_next.astype(jnp.int32) + across_prev.astype(jnp.int32))

    send_halo(0)

    for c in range(per):
        for h in range(c * group, (c + 1) * group):
            if h >= EARLY:
                state(h)

        @pl.when(jnp.logical_not(late))
        def _(c=c):
            send_states(c)

    lane_head = lax.broadcasted_iota(jnp.int32, (tok, heads * width), 1) // width
    load_qf.wait()
    kt_narrow = kt[...].astype(BF16)
    q_quarter = qf[...] * jnp.asarray(0.25, BF16)
    diagonal = (lax.broadcasted_iota(jnp.int32, (TILE, TILE), 0)
                >= lax.broadcasted_iota(jnp.int32, (TILE, TILE), 1))

    def scores(h):
        lone = jnp.where(lane_head == h, q_quarter, jnp.zeros_like(q_quarter))
        for i in range(tiles):
            t0 = i * TILE
            reach = t0 + TILE
            x = dot(lone[t0:reach, :], kt_narrow[:, 0:reach])
            poly = 1.0 + x * (1.0 + 0.5 * x)
            gap = ccol[t0:reach, h:h + 1] - crow[h:h + 1, 0:reach]
            last = jnp.where(diagonal, gap[:, t0:reach], -1e30)
            if i > 0:
                gap = jnp.concatenate([gap[:, 0:t0], last], axis=1)
            else:
                gap = last
            score = (poly * jnp.exp(gap)).astype(BF16)
            numden[h, t0:reach, :] = dot(score, vw[h, 0:reach, :])

    def fade_of(slab):
        return slab[MIX:MIX + 1, FADE_HI:FADE_HI + 1] + slab[MIX:MIX + 1, FADE_LO:FADE_LO + 1]

    def across(c, slab, last_slab):
        lanes = pl.ds(pl.multiple_of((c * group + r) * size, size), size)
        taps = weight[:, lanes]
        last = last_slab.astype(F32)
        last_1, last_2 = last[LAST_1:LAST_1 + 1, :], last[LAST_2:LAST_2 + 1, :]
        change_0 = taps[1:2, :] * last_1 + taps[2:3, :] * last_2
        change_1 = taps[2:3, :] * last_1
        at_a = jnp.where(slab_row == KEY_0, change_0, jnp.where(slab_row == KEY_1, change_1, 0.0))
        at_0 = jnp.where(slab_row == MIX, change_0, 0.0)
        at_1 = jnp.where(slab_row == MIX, change_1, 0.0)
        out = dot_first(slab, jnp.concatenate([at_a, at_0, at_1], axis=1).astype(BF16))
        rest = out[REST:2 * REST, size:2 * size] + out[2 * REST:3 * REST, 2 * size:3 * size]
        return jnp.concatenate([out[:, 0:size], rest], axis=0)

    def emit(c, earlier):
        def entering(i):
            e = e_group[c, i]
            return (e if earlier is None else e + faded[c * group + i] * earlier).astype(BF16)

        for turn in range(1, group):
            target = turned(turn)
            e_send[c, target] = entering(target)
            e_copy(c, target).start()
        e_recv[c * group + r] = entering(r)

    def gather(c):
        for turn in range(1, group):
            s_arrival(c, turned(turn)).wait_recv()
        running = jnp.zeros((FOLDED, size), F32)
        fades = jnp.ones((1, size), F32)

        def step(j, running, fades):
            block = s_recv[c, j].astype(F32)
            fade = fade_of(block[SLAB:SLAB + 16, :])
            running = fade * running + block
            if j > 0:
                running = running + across(
                    c, s_recv[c, j, SLAB:SLAB + 16, :], s_recv[c, j - 1, SLAB:SLAB + 16, :])
            return running, fades * fade

        for j in range(group - 1):
            e_group[c, j] = running
            faded[c * group + j] = fades
            running, fades = step(j, running, fades)
        e_group[c, group - 1] = running
        faded[c * group + group - 1] = fades

        @pl.when(g < groups - 1)
        def _():
            total, whole = step(group - 1, running, fades)
            whole_hi = whole.astype(BF16).astype(F32)
            slab = total[SLAB:SLAB + 16, :]
            slab = jnp.where((slab_row == MIX) & (slab_lane >= FADE_HI), whole_hi, slab)
            slab = jnp.where((slab_row == MIX) & (slab_lane >= FADE_LO), whole - whole_hi, slab)
            t_send[c] = jnp.concatenate(
                [total[0:SLAB, :], slab, total[SLAB + 16:, :]], axis=0).astype(BF16)
            for target in range(1, groups):
                @pl.when(target > g)
                def _(target=target):
                    t_copy(c, target).start()

    def first_group():
        @pl.when(g == 0)
        def _():
            for c in range(per):
                emit(c, None)

    def pass_on(c):
        @pl.when(g > 0)
        def _():
            t_arrival(c, 0).wait_recv()
            before_group[...] = t_recv[c, 0].astype(F32)
            for source in range(1, groups - 1):
                @pl.when(source < g)
                def _(source=source):
                    t_arrival(c, source).wait_recv()
                    block = t_recv[c, source].astype(F32)
                    before_group[...] = fade_of(block[SLAB:SLAB + 16, :]) * before_group[...] + block
            emit(c, before_group[...])

    row = lax.broadcasted_iota(jnp.int32, (WINDOW, 2 * WINDOW), 0)
    col = lax.broadcasted_iota(jnp.int32, (WINDOW, 2 * WINDOW), 1)
    band = (col > row) & (col <= row + WINDOW)
    steps = tok // WINDOW
    scale = size ** (-0.5)
    ones = jnp.ones((2 * WINDOW, size), BF16)

    def slide(h, start, stop, bias):
        lanes = slice(h * size, (h + 1) * size)
        s = jnp.concatenate([
            dot_t(wq[i * WINDOW:(i + 1) * WINDOW, lanes], kx[i * WINDOW:(i + 2) * WINDOW, lanes])
            for i in range(start, stop)], axis=0)
        s = s * scale + bias
        p = jnp.exp(s - jnp.max(s, axis=1, keepdims=True)).astype(BF16)
        pv = jnp.concatenate([
            dot(p[(i - start) * WINDOW:(i - start + 1) * WINDOW, :],
                jnp.concatenate([vx[i * WINDOW:(i + 2) * WINDOW, lanes], ones], axis=1))
            for i in range(start, stop)], axis=0)
        win[start * WINDOW:stop * WINDOW, lanes] = pv[:, 0:size] * inverse(pv[:, size:2 * size])

    @pl.when((me < n - 1) & (lax.axis_index("head") == 0))
    def _():
        for piece in (1, 2, 3,):
            halo_copy(piece).start()

    load_k.wait()
    load_q.wait()
    bias = jnp.concatenate([jnp.where(band, 0.0, -1e30)] * (steps - 1), axis=0)
    for h in range(0, 1):
        slide(h, 1, steps, bias)

    @pl.when(late)
    def _():
        first = first_rows()
        for h in range(heads):
            change = jnp.concatenate(
                [correct(h, first).astype(BF16), jnp.zeros((TILE - 16, size), BF16)], axis=0)
            s_send[h] = (s_send[h].astype(F32) + dot(phik[h, :, 0:TILE], change)).astype(BF16)
        for c in range(per):
            send_states(c)

    for c in range(per):
        s_recv[c, r] = s_send[c * group + r]

    @pl.when((me < n - 1) & (lax.axis_index("head") == 0))
    def _():
        for piece in (4, 5,):
            halo_copy(piece).start()

    for h in range(1, 2):
        slide(h, 1, steps, bias)

    @pl.when((me < n - 1) & (lax.axis_index("head") == 0))
    def _():
        for piece in (6, 7,):
            halo_copy(piece).start()

    for h in range(2, 4):
        slide(h, 1, steps, bias)

    @pl.when((me < n - 1) & (lax.axis_index("head") == 1))
    def _():
        for piece in (1, 2,):
            halo_copy(piece).start()

    for h in range(4, 6):
        slide(h, 1, steps, bias)

    @pl.when((me < n - 1) & (lax.axis_index("head") == 1))
    def _():
        for piece in (3, 4,):
            halo_copy(piece).start()

    for h in range(6, 8):
        slide(h, 1, steps, bias)

    @pl.when((me > 0) & jnp.logical_not(late))
    def _():
        first = first_rows()
        for h in range(heads):
            correct(h, first)

    @pl.when((me < n - 1) & (lax.axis_index("head") == 1))
    def _():
        for piece in (5,):
            halo_copy(piece).start()

    for h in range(0, 1):
        scores(h)

    @pl.when((me < n - 1) & (lax.axis_index("head") == 1))
    def _():
        for piece in (6, 7,):
            halo_copy(piece).start()

    for h in range(1, 5):
        scores(h)

    gather(0)

    gather(1)

    first_group()

    for h in range(5, 7):
        scores(h)

    pass_on(0)

    qt[...] = qf[...].astype(F32).T
    entering = jnp.exp(crow[...])
    for h in range(heads):
        phiq[h] = fold_features(
            qt[h * width:(h + 1) * width, :], entering[h:h + 1, :], 1.0 / 32, 1.0 / 16, 0.25).T

    pass_on(1)

    for h in range(7, 8):
        scores(h)

    @pl.when(me > 0)
    def _():
        for which in range(1, 2 * pieces):
            halo_copy(which).wait_recv()

    first_bias = jnp.where(band & ((col >= WINDOW) | (me > 0)), 0.0, -1e30)
    for h in range(heads):
        slide(h, 0, 1, first_bias)

    picks = jnp.concatenate(
        [jnp.where(slab_row == at, 1.0, 0.0) for at in (NORM, MIX)], axis=1).astype(BF16)
    def finish_head(h):
        lanes = pl.ds(pl.multiple_of(h * size, size), size)
        before = e_recv[h]
        norm = dot_first(before[SLAB:SLAB + 16, :], picks)
        norm = jnp.concatenate([norm[:, 0:size], norm[0:REST, size:2 * size]], axis=0).astype(BF16)
        both = numden[h] + dot(phiq[h], jnp.concatenate([before, norm], axis=1))
        out[:, lanes] = (both[:, 0:size] * inverse(both[:, size:2 * size]) + win[:, lanes]).astype(BF16)

    for c in range(per):
        finish_head(c * group + r)
    for c in range(per):
        for turn in range(1, group):
            e_arrival(c * group + turned(turn)).wait_recv()
        for turn in range(1, group):
            finish_head(c * group + turned(turn))

    @pl.when(me < n - 1)
    def _():
        for which in range(2 * pieces):
            halo_copy(which).wait_send()

    for c in range(per):
        for turn in range(1, group):
            s_copy(c, turned(turn)).wait_send()
            e_copy(c, turned(turn)).wait_send()

        for target in range(1, groups):
            @pl.when(target > g)
            def _(target=target, c=c):
                t_copy(c, target).wait_send()


def solution(mesh):
    n = mesh.shape["seq"]

    def local(q_feat, k_feat, values, win_query, win_key, log_gates, conv_weight):
        tok, channels = values.shape
        heads = log_gates.shape[1]
        size = channels // heads
        width = q_feat.shape[1] // heads
        group = next(s for s in (4, 2, 1) if n % s == 0 and heads % s == 0)
        groups, per = n // group, heads // group
        hbm = pl.BlockSpec(memory_space=pltpu.HBM)
        dma = pltpu.SemaphoreType.DMA
        block = (FOLDED, size)
        operands = (q_feat, k_feat, log_gates.T, conv_weight, values, win_key, win_query)
        return pl.pallas_call(
            functools.partial(kernel, n, group, heads, size, width),
            out_shape=jax.ShapeDtypeStruct((tok, channels), BF16),
            in_specs=[hbm] * 7,
            out_specs=pl.BlockSpec(memory_space=pltpu.VMEM),
            scratch_shapes=[
                pltpu.VMEM(q_feat.shape, BF16),
                pltpu.VMEM(k_feat.shape, BF16),
                pltpu.VMEM((heads, tok), F32),
                pltpu.VMEM(conv_weight.shape, F32),
                pltpu.VMEM((tok + WINDOW, channels), BF16),
                pltpu.VMEM((tok + WINDOW, channels), BF16),
                pltpu.VMEM((tok, channels), BF16),
                pltpu.VMEM((tok + 8, channels), F32),
                pltpu.VMEM((heads, tok, 2 * size), BF16),
                pltpu.VMEM((heads * width, tok), F32),
                pltpu.VMEM((heads * width, tok), F32),
                pltpu.VMEM((heads, FOLDED, tok), BF16),
                pltpu.VMEM((heads, tok, FOLDED), BF16),
                pltpu.VMEM((heads, tok, 2 * size), F32),
                pltpu.VMEM((tok, channels), F32),
                pltpu.VMEM((tok, 128), F32),
                pltpu.VMEM((heads, tok), F32),
                pltpu.VMEM((heads,) + block, BF16),
                pltpu.VMEM((per, group) + block, BF16),
                pltpu.VMEM((per, group) + block, F32),
                pltpu.VMEM((heads, 1, size), F32),
                pltpu.VMEM(block, F32),
                pltpu.VMEM((per,) + block, BF16),
                pltpu.VMEM((per, groups) + block, BF16),
                pltpu.VMEM((per, group) + block, BF16),
                pltpu.VMEM((heads,) + block, BF16),
                dma((7,)), dma((2 * WINDOW // PIECE,)), dma((2 * WINDOW // PIECE,)),
                dma((heads,)), dma((per, group)), dma((per, groups)), dma((per, groups)),
                dma((per, group)), dma((heads,)),
            ],
            compiler_params=pltpu.CompilerParams(
                collective_id=0, has_side_effects=True, vmem_limit_bytes=40 * 1024 * 1024),
        )(*[pltpu.with_memory_space_constraint(x, pltpu.HBM) for x in operands])

    shard = P(("grp", "seq"), "head")
    return jax.shard_map(
        local, mesh=mesh, in_specs=(shard,) * 6 + (P(None, "head"),), out_specs=shard, check_vma=False)
```

```python
import functools

import jax
import jax.numpy as jnp
from jax import lax
from jax.experimental import pallas as pl
from jax.experimental.pallas import tpu as pltpu
from jax.sharding import PartitionSpec as P

WINDOW = 64
TILE = 128
FOLDED = 160
SLAB = 128
NORM, KEY_0, KEY_1, MIX, LAST_2, LAST_1 = 9, 10, 11, 12, 13, 14
REST = FOLDED - SLAB
FADE_HI, FADE_LO = 96, 112
EARLY = 4
PIECE = 16
F32 = jnp.float32
BF16 = jnp.bfloat16
MESH = pl.DeviceIdType.MESH


def dot(a, b):
    return lax.dot_general(a, b, (((1,), (0,)), ((), ())), preferred_element_type=F32)


def dot_t(a, b):
    return lax.dot_general(a, b, (((1,), (1,)), ((), ())), preferred_element_type=F32)


def dot_first(a, b):
    return lax.dot_general(a, b, (((0,), (0,)), ((), ())), preferred_element_type=F32)


def inverse(x):
    guess = pl.reciprocal(x, approx=True)
    return guess * (2.0 - x * guess)


def fold_features(x, level, square_scale, pair_scale, linear_scale):
    rows = lax.broadcasted_iota(jnp.int32, x.shape, 0)
    levelled = x * level
    scaled = levelled * pair_scale
    parts = [(levelled * square_scale) * x]
    for step in range(1, 8):
        parts.append(scaled * pltpu.roll(x, 16 - step, 0))
    half = scaled * pltpu.roll(x, 8, 0)
    parts.append(jnp.where(rows < 8, half, jnp.where(rows == 8, level, 0.0)))
    parts.append(levelled * linear_scale)
    return jnp.concatenate([part.astype(BF16) for part in parts], axis=0)


def kernel(
    n, group, heads, size, width,
    q_feat, k_feat, log_gates, conv_weight, values, win_key, win_query,
    out,
    qf, kf, gates, weight,
    vx, kx, wq, vf, vw, qt, kt, phik, phiq, numden, win, ccol, crow,
    s_send, s_recv, e_group, faded, before_group, t_send, t_recv, e_send, e_recv,
    in_sem, halo_send, halo_recv, ss_sem, sr_sem, ts_sem, tr_sem, es_sem, er_sem,
):
    me = lax.axis_index("seq")
    groups = n // group
    per = heads // group
    g = me // group
    r = lax.rem(me, group)
    tok = qf.shape[0]
    tiles = tok // TILE
    tail = WINDOW
    pieces = tail // PIECE

    loads = [
        pltpu.make_async_copy(log_gates, gates, in_sem.at[0]),
        pltpu.make_async_copy(k_feat, kf, in_sem.at[1]),
        pltpu.make_async_copy(values, vx.at[pl.ds(tail, tok)], in_sem.at[2]),
        pltpu.make_async_copy(conv_weight, weight, in_sem.at[3]),
        pltpu.make_async_copy(q_feat, qf, in_sem.at[4]),
        pltpu.make_async_copy(win_key, kx.at[pl.ds(tail, tok)], in_sem.at[5]),
        pltpu.make_async_copy(win_query, wq, in_sem.at[6]),
    ]
    for load in loads[:5]:
        load.start()
    load_g, load_kf, load_v, load_w, load_qf, load_k, load_q = loads

    barrier = pltpu.get_barrier_semaphore()

    def greet(peer):
        pl.semaphore_signal(barrier, inc=1, device_id={"seq": peer}, device_id_type=MESH)

    for turn in range(1, group):
        greet(g * group + lax.rem(r + turn, group))
    for turn in range(1, groups):
        greet(lax.rem(me + turn * group, n))
    across_next = (r == group - 1) & (g < groups - 1)
    across_prev = (r == 0) & (g > 0)

    @pl.when(across_next)
    def _():
        greet(me + 1)

    @pl.when(across_prev)
    def _():
        greet(me - 1)

    @pl.when(me == 0)
    def _():
        vx[0:tail, :] = jnp.zeros((tail, heads * size), BF16)
        kx[0:tail, :] = jnp.zeros((tail, heads * size), BF16)

    vf[0:8, :] = jnp.zeros((8, heads * size), F32)
    nxt = lax.rem(me + 1, n)

    def halo_copy(which):
        source, target = ((values, vx), (win_key, kx))[which // pieces]
        start = tail - PIECE * (which % pieces + 1)
        return pltpu.make_async_remote_copy(
            source.at[pl.ds(tok - tail + start, PIECE)], target.at[pl.ds(start, PIECE)],
            halo_send.at[which], halo_recv.at[which], device_id={"seq": nxt}, device_id_type=MESH)

    def send_halo(*which):
        @pl.when(me < n - 1)
        def _():
            for piece in which:
                halo_copy(piece).start()

    def turned(turn):
        return lax.rem(r + turn, group)

    def s_copy(c, owner):
        return pltpu.make_async_remote_copy(
            s_send.at[c * group + owner], s_recv.at[c, r], ss_sem.at[c * group + owner], sr_sem.at[c, r],
            device_id={"seq": g * group + owner}, device_id_type=MESH)

    def s_arrival(c, source):
        return pltpu.make_async_remote_copy(
            s_send.at[c * group], s_recv.at[c, source], ss_sem.at[c * group], sr_sem.at[c, source],
            device_id={"seq": g * group + source}, device_id_type=MESH)

    def t_copy(c, target):
        return pltpu.make_async_remote_copy(
            t_send.at[c], t_recv.at[c, g], ts_sem.at[c, target], tr_sem.at[c, g],
            device_id={"seq": target * group + r}, device_id_type=MESH)

    def t_arrival(c, source):
        return pltpu.make_async_remote_copy(
            t_send.at[c], t_recv.at[c, source], ts_sem.at[c, source], tr_sem.at[c, source],
            device_id={"seq": source * group + r}, device_id_type=MESH)

    def e_copy(c, target):
        return pltpu.make_async_remote_copy(
            e_send.at[c, target], e_recv.at[c * group + r], es_sem.at[c, target], er_sem.at[c * group + r],
            device_id={"seq": g * group + target}, device_id_type=MESH)

    def e_arrival(h):
        return pltpu.make_async_remote_copy(
            e_send.at[0, 0], e_recv.at[h], es_sem.at[0, 0], er_sem.at[h],
            device_id={"seq": g * group + lax.rem(h, group)}, device_id_type=MESH)

    before_or_at = jnp.where(
        lax.broadcasted_iota(jnp.int32, (tok, tok), 0) <= lax.broadcasted_iota(jnp.int32, (tok, tok), 1),
        1.0, 0.0).astype(BF16)
    load_g.wait()
    upper = gates[...].astype(BF16)
    rest = gates[...] - upper.astype(F32)
    middle = rest.astype(BF16)
    lowest = (rest - middle.astype(F32)).astype(BF16)
    total = dot(jnp.concatenate([upper, middle, lowest], axis=0), before_or_at)
    total = total[0:heads] + (total[heads:2 * heads] + total[2 * heads:3 * heads])
    crow[...] = total
    ccol[...] = jnp.concatenate([total, jnp.zeros((128 - heads, tok), F32)], axis=0).T
    keep_row = jnp.exp(total[:, tok - 1:tok] - total)
    finish = jnp.exp(total[:, tok - 1:tok])
    finish_hi = finish.astype(BF16).astype(F32)
    finish_lo = finish - finish_hi

    load_kf.wait()
    kt[...] = kf[...].astype(F32).T
    for h in range(heads):
        phik[h] = fold_features(
            kt[h * width:(h + 1) * width, :], keep_row[h:h + 1, :], 1.0, 1.0, 1.0)

    load_w.wait()
    load_v.wait()
    loads[5].start()
    loads[6].start()
    slab_row = lax.broadcasted_iota(jnp.int32, (16, size), 0)
    slab_lane = lax.broadcasted_iota(jnp.int32, (16, size), 1)
    probe_row = lax.broadcasted_iota(jnp.int32, (16, tok), 0)
    probe_lane = lax.broadcasted_iota(jnp.int32, (16, tok), 1)
    probes = jnp.where((probe_row == 0) | (probe_lane == probe_row - 1), 1.0, 0.0).astype(BF16)
    late = (r == 0) & (g > 0)

    def state(h):
        lanes = slice(h * size, (h + 1) * size)
        current = vx[tail:tail + tok, lanes].astype(F32)
        vf[8:8 + tok, lanes] = current
        conv = weight[0:1, lanes] * current
        for tap in range(1, weight.shape[0]):
            conv = conv + weight[tap:tap + 1, lanes] * vf[8 - tap:8 - tap + tok, lanes]
        conv = conv.astype(BF16)
        vw[h, :, 0:size] = conv
        vw[h, :, size:2 * size] = jnp.ones((tok, size), BF16)
        folded = dot(phik[h], conv)
        probed = dot_t(probes, phik[h])
        ends = jnp.concatenate([probed[:, SLAB:FOLDED], jnp.zeros((16, SLAB - REST), F32)], axis=1)
        mix = (ends[0:1, :] + pltpu.roll(ends, REST, 1)[1:2, :] + pltpu.roll(ends, 2 * REST, 1)[2:3, :])
        mix = jnp.where(slab_lane[0:1, :] >= FADE_HI, finish_hi[h:h + 1, :], mix)
        mix = jnp.where(slab_lane[0:1, :] >= FADE_LO, finish_lo[h:h + 1, :], mix)
        slab = folded[SLAB:SLAB + 16, :]
        for at, line in ((NORM, probed[0:1, 0:SLAB]), (KEY_0, probed[1:2, 0:SLAB]), (KEY_1, probed[2:3, 0:SLAB]),
                         (MIX, mix), (LAST_2, current[tok - 2:tok - 1, :]), (LAST_1, current[tok - 1:tok, :])):
            slab = jnp.where(slab_row == at, line, slab)
        s_send[h] = jnp.concatenate([folded[0:SLAB, :], slab, folded[SLAB + 16:, :]], axis=0).astype(BF16)

    def send_states(c):
        for turn in range(1, group):
            s_copy(c, turned(turn)).start()

    def correct(h, first):
        lanes = slice(h * size, (h + 1) * size)
        change = first[:, lanes].astype(F32) - vw[h, 0:16, 0:size].astype(F32)
        vw[h, 0:16, 0:size] = first[:, lanes]
        return change

    def first_rows():
        halo_copy(0).wait_recv()
        vf[0:8, :] = vx[tail - 16:tail, :].astype(F32)[8:16, :]
        first = weight[0:1, :] * vf[8:24, :]
        for tap in range(1, weight.shape[0]):
            first = first + weight[tap:tap + 1, :] * vf[8 - tap:24 - tap, :]
        return first.astype(BF16)

    for h in range(EARLY):
        state(h)
    pl.semaphore_wait(
        barrier, (group - 1) + (groups - 1) + across_next.astype(jnp.int32) + across_prev.astype(jnp.int32))

    send_halo(0)

    for c in range(per):
        for h in range(c * group, (c + 1) * group):
            if h >= EARLY:
                state(h)

        @pl.when(jnp.logical_not(late))
        def _(c=c):
            send_states(c)

    lane_head = lax.broadcasted_iota(jnp.int32, (tok, heads * width), 1) // width
    load_qf.wait()
    kt_narrow = kt[...].astype(BF16)
    q_quarter = qf[...] * jnp.asarray(0.25, BF16)
    diagonal = (lax.broadcasted_iota(jnp.int32, (TILE, TILE), 0)
                >= lax.broadcasted_iota(jnp.int32, (TILE, TILE), 1))

    def scores(h):
        lone = jnp.where(lane_head == h, q_quarter, jnp.zeros_like(q_quarter))
        for i in range(tiles):
            t0 = i * TILE
            reach = t0 + TILE
            x = dot(lone[t0:reach, :], kt_narrow[:, 0:reach])
            poly = 1.0 + x * (1.0 + 0.5 * x)
            gap = ccol[t0:reach, h:h + 1] - crow[h:h + 1, 0:reach]
            last = jnp.where(diagonal, gap[:, t0:reach], -1e30)
            if i > 0:
                gap = jnp.concatenate([gap[:, 0:t0], last], axis=1)
            else:
                gap = last
            score = (poly * jnp.exp(gap)).astype(BF16)
            numden[h, t0:reach, :] = dot(score, vw[h, 0:reach, :])

    def fade_of(slab):
        return slab[MIX:MIX + 1, FADE_HI:FADE_HI + 1] + slab[MIX:MIX + 1, FADE_LO:FADE_LO + 1]

    def across(c, slab, last_slab):
        lanes = pl.ds(pl.multiple_of((c * group + r) * size, size), size)
        taps = weight[:, lanes]
        last = last_slab.astype(F32)
        last_1, last_2 = last[LAST_1:LAST_1 + 1, :], last[LAST_2:LAST_2 + 1, :]
        change_0 = taps[1:2, :] * last_1 + taps[2:3, :] * last_2
        change_1 = taps[2:3, :] * last_1
        at_a = jnp.where(slab_row == KEY_0, change_0, jnp.where(slab_row == KEY_1, change_1, 0.0))
        at_0 = jnp.where(slab_row == MIX, change_0, 0.0)
        at_1 = jnp.where(slab_row == MIX, change_1, 0.0)
        out = dot_first(slab, jnp.concatenate([at_a, at_0, at_1], axis=1).astype(BF16))
        rest = out[REST:2 * REST, size:2 * size] + out[2 * REST:3 * REST, 2 * size:3 * size]
        return jnp.concatenate([out[:, 0:size], rest], axis=0)

    def emit(c, earlier):
        def entering(i):
            e = e_group[c, i]
            return (e if earlier is None else e + faded[c * group + i] * earlier).astype(BF16)

        for turn in range(1, group):
            target = turned(turn)
            e_send[c, target] = entering(target)
            e_copy(c, target).start()
        e_recv[c * group + r] = entering(r)

    def gather(c):
        for turn in range(1, group):
            s_arrival(c, turned(turn)).wait_recv()
        running = jnp.zeros((FOLDED, size), F32)
        fades = jnp.ones((1, size), F32)

        def step(j, running, fades):
            block = s_recv[c, j].astype(F32)
            fade = fade_of(block[SLAB:SLAB + 16, :])
            running = fade * running + block
            if j > 0:
                running = running + across(
                    c, s_recv[c, j, SLAB:SLAB + 16, :], s_recv[c, j - 1, SLAB:SLAB + 16, :])
            return running, fades * fade

        for j in range(group - 1):
            e_group[c, j] = running
            faded[c * group + j] = fades
            running, fades = step(j, running, fades)
        e_group[c, group - 1] = running
        faded[c * group + group - 1] = fades

        @pl.when(g < groups - 1)
        def _():
            total, whole = step(group - 1, running, fades)
            whole_hi = whole.astype(BF16).astype(F32)
            slab = total[SLAB:SLAB + 16, :]
            slab = jnp.where((slab_row == MIX) & (slab_lane >= FADE_HI), whole_hi, slab)
            slab = jnp.where((slab_row == MIX) & (slab_lane >= FADE_LO), whole - whole_hi, slab)
            t_send[c] = jnp.concatenate(
                [total[0:SLAB, :], slab, total[SLAB + 16:, :]], axis=0).astype(BF16)
            for target in range(1, groups):
                @pl.when(target > g)
                def _(target=target):
                    t_copy(c, target).start()

    def first_group():
        @pl.when(g == 0)
        def _():
            for c in range(per):
                emit(c, None)

    def pass_on(c):
        @pl.when(g > 0)
        def _():
            t_arrival(c, 0).wait_recv()
            before_group[...] = t_recv[c, 0].astype(F32)
            for source in range(1, groups - 1):
                @pl.when(source < g)
                def _(source=source):
                    t_arrival(c, source).wait_recv()
                    block = t_recv[c, source].astype(F32)
                    before_group[...] = fade_of(block[SLAB:SLAB + 16, :]) * before_group[...] + block
            emit(c, before_group[...])

    row = lax.broadcasted_iota(jnp.int32, (WINDOW, 2 * WINDOW), 0)
    col = lax.broadcasted_iota(jnp.int32, (WINDOW, 2 * WINDOW), 1)
    band = (col > row) & (col <= row + WINDOW)
    steps = tok // WINDOW
    scale = size ** (-0.5)
    ones = jnp.ones((2 * WINDOW, size), BF16)

    def slide(h, start, stop, bias):
        lanes = slice(h * size, (h + 1) * size)
        s = jnp.concatenate([
            dot_t(wq[i * WINDOW:(i + 1) * WINDOW, lanes], kx[i * WINDOW:(i + 2) * WINDOW, lanes])
            for i in range(start, stop)], axis=0)
        s = s * scale + bias
        p = jnp.exp(s - jnp.max(s, axis=1, keepdims=True)).astype(BF16)
        pv = jnp.concatenate([
            dot(p[(i - start) * WINDOW:(i - start + 1) * WINDOW, :],
                jnp.concatenate([vx[i * WINDOW:(i + 2) * WINDOW, lanes], ones], axis=1))
            for i in range(start, stop)], axis=0)
        win[start * WINDOW:stop * WINDOW, lanes] = pv[:, 0:size] * inverse(pv[:, size:2 * size])

    @pl.when((me < n - 1) & (lax.axis_index("head") == 0))
    def _():
        for piece in (1, 2, 3,):
            halo_copy(piece).start()

    load_k.wait()
    load_q.wait()
    bias = jnp.concatenate([jnp.where(band, 0.0, -1e30)] * (steps - 1), axis=0)
    for h in range(0, 1):
        slide(h, 1, steps, bias)

    @pl.when((me < n - 1) & (lax.axis_index("head") == 0))
    def _():
        for piece in (4, 5,):
            halo_copy(piece).start()

    for h in range(1, 2):
        slide(h, 1, steps, bias)

    @pl.when(late)
    def _():
        first = first_rows()
        for h in range(heads):
            change = jnp.concatenate(
                [correct(h, first).astype(BF16), jnp.zeros((TILE - 16, size), BF16)], axis=0)
            s_send[h] = (s_send[h].astype(F32) + dot(phik[h, :, 0:TILE], change)).astype(BF16)
        for c in range(per):
            send_states(c)

    for c in range(per):
        s_recv[c, r] = s_send[c * group + r]

    @pl.when((me < n - 1) & (lax.axis_index("head") == 0))
    def _():
        for piece in (6, 7,):
            halo_copy(piece).start()

    for h in range(2, 4):
        slide(h, 1, steps, bias)

    @pl.when((me < n - 1) & (lax.axis_index("head") == 1))
    def _():
        for piece in (1, 2,):
            halo_copy(piece).start()

    for h in range(4, 6):
        slide(h, 1, steps, bias)

    @pl.when((me < n - 1) & (lax.axis_index("head") == 1))
    def _():
        for piece in (3, 4,):
            halo_copy(piece).start()

    for h in range(6, 8):
        slide(h, 1, steps, bias)

    @pl.when((me > 0) & jnp.logical_not(late))
    def _():
        first = first_rows()
        for h in range(heads):
            correct(h, first)

    @pl.when((me < n - 1) & (lax.axis_index("head") == 1))
    def _():
        for piece in (5,):
            halo_copy(piece).start()

    for h in range(0, 1):
        scores(h)

    @pl.when((me < n - 1) & (lax.axis_index("head") == 1))
    def _():
        for piece in (6, 7,):
            halo_copy(piece).start()

    for h in range(1, 5):
        scores(h)

    gather(0)

    gather(1)

    first_group()

    for h in range(5, 7):
        scores(h)

    pass_on(0)

    qt[...] = qf[...].astype(F32).T
    entering = jnp.exp(crow[...])
    for h in range(heads):
        phiq[h] = fold_features(
            qt[h * width:(h + 1) * width, :], entering[h:h + 1, :], 1.0 / 32, 1.0 / 16, 0.25).T

    pass_on(1)

    for h in range(7, 8):
        scores(h)

    @pl.when(me > 0)
    def _():
        for which in range(1, 2 * pieces):
            halo_copy(which).wait_recv()

    first_bias = jnp.where(band & ((col >= WINDOW) | (me > 0)), 0.0, -1e30)
    for h in range(heads):
        slide(h, 0, 1, first_bias)

    picks = jnp.concatenate(
        [jnp.where(slab_row == at, 1.0, 0.0) for at in (NORM, MIX)], axis=1).astype(BF16)
    def finish_head(h):
        lanes = pl.ds(pl.multiple_of(h * size, size), size)
        before = e_recv[h]
        norm = dot_first(before[SLAB:SLAB + 16, :], picks)
        norm = jnp.concatenate([norm[:, 0:size], norm[0:REST, size:2 * size]], axis=0).astype(BF16)
        both = numden[h] + dot(phiq[h], jnp.concatenate([before, norm], axis=1))
        out[:, lanes] = (both[:, 0:size] * inverse(both[:, size:2 * size]) + win[:, lanes]).astype(BF16)

    for c in range(per):
        finish_head(c * group + r)
    for c in range(per):
        for turn in range(1, group):
            e_arrival(c * group + turned(turn)).wait_recv()
        for turn in range(1, group):
            finish_head(c * group + turned(turn))

    @pl.when(me < n - 1)
    def _():
        for which in range(2 * pieces):
            halo_copy(which).wait_send()

    for c in range(per):
        for turn in range(1, group):
            s_copy(c, turned(turn)).wait_send()
            e_copy(c, turned(turn)).wait_send()

        for target in range(1, groups):
            @pl.when(target > g)
            def _(target=target, c=c):
                t_copy(c, target).wait_send()


def solution(mesh):
    n = mesh.shape["seq"]

    def local(q_feat, k_feat, values, win_query, win_key, log_gates, conv_weight):
        tok, channels = values.shape
        heads = log_gates.shape[1]
        size = channels // heads
        width = q_feat.shape[1] // heads
        group = next(s for s in (4, 2, 1) if n % s == 0 and heads % s == 0)
        groups, per = n // group, heads // group
        hbm = pl.BlockSpec(memory_space=pltpu.HBM)
        dma = pltpu.SemaphoreType.DMA
        block = (FOLDED, size)
        operands = (q_feat, k_feat, log_gates.T, conv_weight, values, win_key, win_query)
        return pl.pallas_call(
            functools.partial(kernel, n, group, heads, size, width),
            out_shape=jax.ShapeDtypeStruct((tok, channels), BF16),
            in_specs=[hbm] * 7,
            out_specs=pl.BlockSpec(memory_space=pltpu.VMEM),
            scratch_shapes=[
                pltpu.VMEM(q_feat.shape, BF16),
                pltpu.VMEM(k_feat.shape, BF16),
                pltpu.VMEM((heads, tok), F32),
                pltpu.VMEM(conv_weight.shape, F32),
                pltpu.VMEM((tok + WINDOW, channels), BF16),
                pltpu.VMEM((tok + WINDOW, channels), BF16),
                pltpu.VMEM((tok, channels), BF16),
                pltpu.VMEM((tok + 8, channels), F32),
                pltpu.VMEM((heads, tok, 2 * size), BF16),
                pltpu.VMEM((heads * width, tok), F32),
                pltpu.VMEM((heads * width, tok), F32),
                pltpu.VMEM((heads, FOLDED, tok), BF16),
                pltpu.VMEM((heads, tok, FOLDED), BF16),
                pltpu.VMEM((heads, tok, 2 * size), F32),
                pltpu.VMEM((tok, channels), F32),
                pltpu.VMEM((tok, 128), F32),
                pltpu.VMEM((heads, tok), F32),
                pltpu.VMEM((heads,) + block, BF16),
                pltpu.VMEM((per, group) + block, BF16),
                pltpu.VMEM((per, group) + block, F32),
                pltpu.VMEM((heads, 1, size), F32),
                pltpu.VMEM(block, F32),
                pltpu.VMEM((per,) + block, BF16),
                pltpu.VMEM((per, groups) + block, BF16),
                pltpu.VMEM((per, group) + block, BF16),
                pltpu.VMEM((heads,) + block, BF16),
                dma((7,)), dma((2 * WINDOW // PIECE,)), dma((2 * WINDOW // PIECE,)),
                dma((heads,)), dma((per, group)), dma((per, groups)), dma((per, groups)),
                dma((per, group)), dma((heads,)),
            ],
            compiler_params=pltpu.CompilerParams(
                collective_id=0, has_side_effects=True, vmem_limit_bytes=40 * 1024 * 1024),
        )(*[pltpu.with_memory_space_constraint(x, pltpu.HBM) for x in operands])

    shard = P(("grp", "seq"), "head")
    return jax.shard_map(
        local, mesh=mesh, in_specs=(shard,) * 6 + (P(None, "head"),), out_specs=shard, check_vma=False)
```
